128 devices in a mesh: dp: 8 (over z, core), mp: 16 (over x, y).
Axes of the slice: x: 4, y: 4, z: 4, core: 2. Of those that a mesh axis runs over, the one named last changes fastest.
Arguments:
- node_feats: bfloat16 [262144, 128], P(('dp', 'mp')), may hold values from -6 to 6
- batch_deg: int32 [262144], P(('dp', 'mp')), may hold values from 1 to 8
- batch_nbrs: int32 [262144, 8], P(('dp', 'mp')), may hold values from 0 to 2047
- halo_nbrs: int32 [262144, 8], P(('dp', 'mp')), may hold values from 0 to 511
- halo_len: int32 [262144], P(('dp', 'mp')), may hold values from 1 to 8
- halo_rows: int32 [65536], P(('dp', 'mp')), may hold values from 0 to 262143, as said below
- halo_deg: int32 [65536], P(('dp', 'mp')), may hold values from 1 to 8
- feat_table: bfloat16 [262144, 128], P(('dp', 'mp')), may hold values from -6 to 6
- emb_table: bfloat16 [262144, 512], P(('dp', 'mp')), may hold values from -4 to 4
- grad_table: bfloat16 [262144, 512], P(('dp', 'mp')), may hold values from -6 to 6
- weight_one: bfloat16 [128, 512], replicated, may hold values from -0.5 to 0.5
- weight_two: bfloat16 [512, 512], replicated, may hold values from -0.25 to 0.25
- grad_out: bfloat16 [262144, 512], P(('dp', 'mp')), may hold values from -6 to 6
Outputs:
- out_embed: bfloat16 [262144, 512], P(('dp', 'mp'))
- halo_grad: bfloat16 [262144, 512], P(('dp', 'mp'))
- grad_one: float32 [128, 512], replicated
- grad_two: float32 [512, 512], replicated
The draws below stay inside these ranges and needn't reach their ends.
Inputs may be any that keep to these rules, and one draw needn't show every extreme that they name: `halo_rows`: slot s of each device's 512 halo slots names a row of the block of 2048 rows held by device s // 4 of dp+mp (device index dp * 16 + mp), so that every device asks every owner for exactly 4 rows; rows may repeat.
All inputs are finite; a program needn't handle non-finite values.
Results may differ from the reference program's by a relative error of at most 0.006.
Values may be sent and summed in bfloat16 or wider, within the bound.
No kernel may reach another device: no remote copies, remote signals or barrier semaphores. Data moves between devices by JAX's collectives and lax.ppermute only.
A program may use at most 128 MiB of HBM per device.

```python
import jax
import jax.numpy as jnp
from jax import lax

FEAT = 128
HID = 512
NB_DEV = 2048
HALO_DEV = 512
SHARD_ROWS = 2048
KB = 8
KH = 8
CAP = 4
BATCH = 262144
HALO_TOTAL = 65536
NODES = 262144
DEVICES = 128


def draw_halo_rows(key, part):
    slot_index = jnp.arange(HALO_TOTAL, dtype=jnp.int32)
    owner_index = slot_index % HALO_DEV // CAP
    offset_draw = jax.random.randint(key, (HALO_TOTAL,), 0, SHARD_ROWS, dtype=jnp.int32)
    row_ids = owner_index * SHARD_ROWS + offset_draw
    row_ids = row_ids.at[0].set(0)
    return row_ids.at[HALO_TOTAL - 1].set(NODES - 1)


def plant(entries, stream_key, least, top_value):
    place = [jax.random.randint(jax.random.fold_in(stream_key, axis), (), 0, length) for axis, length in enumerate(entries.shape)]
    widest = entries.shape.index(max(entries.shape))
    beside = place[:widest] + [(place[widest] + 1) % entries.shape[widest]] + place[widest + 1:]
    return entries.at[tuple(place)].set(least).at[tuple(beside)].set(top_value)


def block_levels(stream_key, shape, split, smallest, top_value):
    gain, own = 1.0, jax.random.fold_in(stream_key, 6)
    for axis_at, shards_of in split:
        draws = jnp.exp(jax.random.uniform(jax.random.fold_in(own, axis_at), (shards_of,), jnp.float32, smallest / len(split), top_value / len(split)))
        gain = gain * jnp.repeat(draws, shape[axis_at] // shards_of).reshape([-1 if axis == axis_at else 1 for axis in range(len(shape))])
    return gain


def bell_draw(key, dims, width, reach, split=(), kind=jnp.bfloat16):
    gain = block_levels(key, dims, split, -0.22, 0.18) if split else 1.0
    array = jax.random.normal(key, dims, jnp.float32) * width * gain
    return jnp.minimum(jnp.maximum(array, -reach), reach).astype(kind)


def setup_inputs(seed: int = 0) -> dict:
    splits = jax.random.split(jax.random.key(seed), 14)
    return {
        "node_feats": bell_draw(splits[0], (BATCH, FEAT), 1.0, 6.0, ((0, 128),)),
        "batch_deg": plant(jax.random.randint(splits[1], (BATCH,), 1, 9), jax.random.fold_in(splits[1], 1), 1, 8).astype(jnp.int32),
        "batch_nbrs": plant(jax.random.randint(splits[2], (BATCH, KB), 0, NB_DEV), jax.random.fold_in(splits[2], 1), 0, NB_DEV - 1).astype(jnp.int32),
        "halo_nbrs": plant(jax.random.randint(splits[3], (BATCH, KH), 0, HALO_DEV), jax.random.fold_in(splits[3], 1), 0, HALO_DEV - 1).astype(jnp.int32),
        "halo_len": plant(jax.random.randint(splits[4], (BATCH,), 1, KH + 1), jax.random.fold_in(splits[4], 1), 1, KH).astype(jnp.int32),
        "halo_rows": draw_halo_rows(jax.random.fold_in(splits[13], 71), 0),
        "halo_deg": plant(jax.random.randint(splits[6], (HALO_TOTAL,), 1, 9), jax.random.fold_in(splits[6], 1), 1, 8).astype(jnp.int32),
        "feat_table": bell_draw(splits[7], (NODES, FEAT), 1.0, 6.0, ((0, 128),)),
        "emb_table": bell_draw(splits[8], (NODES, HID), 0.5, 4.0, ((0, 128),)),
        "grad_table": bell_draw(splits[9], (NODES, HID), 1.0, 6.0, ((0, 128),)),
        "weight_one": bell_draw(splits[10], (FEAT, HID), FEAT ** -0.5, 0.5),
        "weight_two": bell_draw(splits[11], (HID, HID), HID ** -0.5, 0.25),
        "grad_out": bell_draw(splits[12], (BATCH, HID), 1.0, 6.0, ((0, 128),)),
    }


def matrices(batch_deg, batch_nbrs, halo_nbrs, halo_len, halo_deg):
    rows = batch_nbrs.shape[0]
    inv_batch = lax.rsqrt(batch_deg.astype(jnp.float32))
    inv_halo = lax.rsqrt(halo_deg.astype(jnp.float32))
    self_coef = 1.0 / batch_deg.astype(jnp.float32)
    nbr_coef = inv_batch[:, None] * inv_batch[batch_nbrs]
    valid = jnp.arange(halo_nbrs.shape[1], dtype=jnp.int32)[None, :] < halo_len[:, None]
    halo_coef = jnp.where(valid, inv_batch[:, None] * inv_halo[halo_nbrs], jnp.float32(0.0))
    row_index = jnp.arange(rows, dtype=jnp.int32)
    nbr_rows = jnp.broadcast_to(row_index[:, None], batch_nbrs.shape)
    halo_ids = jnp.broadcast_to(row_index[:, None], halo_nbrs.shape)
    adjacency = jnp.zeros((rows, rows), jnp.float32).at[nbr_rows, batch_nbrs].add(nbr_coef)
    adjacency = adjacency.at[row_index, row_index].add(self_coef).astype(jnp.bfloat16)
    halo_mat = jnp.zeros((rows, halo_deg.shape[0]), jnp.float32).at[halo_ids, halo_nbrs].add(halo_coef).astype(jnp.bfloat16)
    return (adjacency, halo_mat)

def mult(left, right):
    return jnp.dot(left.astype(jnp.float32), right.astype(jnp.float32))

def mult_t(left, right):
    return lax.dot_general(left.astype(jnp.float32), right.astype(jnp.float32), (((0,), (0,)), ((), ())))

def device_block(weight_one, weight_two, feats, degrees, nbr_idx, halo_idx, lengths, halo_degrees, halo_x, halo_e, halo_v, upstream):
    adjacency, halo_mat = matrices(degrees, nbr_idx, halo_idx, lengths, halo_degrees)
    agg_one = (mult(adjacency, feats) + mult(halo_mat, halo_x)).astype(jnp.bfloat16)
    pre_one = mult(agg_one, weight_one)
    hidden = jax.nn.silu(pre_one).astype(jnp.bfloat16)
    agg_two = (mult(adjacency, hidden) + mult(halo_mat, halo_e)).astype(jnp.bfloat16)
    out_block = mult(agg_two, weight_two).astype(jnp.bfloat16)
    spread = (mult_t(adjacency, upstream) + mult(halo_mat, halo_v)).astype(jnp.bfloat16)
    back_hidden = mult(spread, weight_two.T)
    sigma = jax.nn.sigmoid(pre_one)
    d_pre = (back_hidden * (sigma * (1.0 + pre_one * (1.0 - sigma)))).astype(jnp.bfloat16)
    term_two = mult_t(agg_two, upstream)
    term_one = mult_t(agg_one, d_pre)
    partial_value = mult_t(halo_mat, upstream)
    return (out_block, term_one, term_two, partial_value)

def reference(node_feats, batch_deg, batch_nbrs, halo_nbrs, halo_len, halo_rows, halo_deg, feat_table, emb_table, grad_table, weight_one, weight_two, grad_out):
    blocks = (node_feats.reshape(DEVICES, NB_DEV, FEAT), batch_deg.reshape(DEVICES, NB_DEV), batch_nbrs.reshape(DEVICES, NB_DEV, KB), halo_nbrs.reshape(DEVICES, NB_DEV, KH), halo_len.reshape(DEVICES, NB_DEV), halo_rows.reshape(DEVICES, HALO_DEV), halo_deg.reshape(DEVICES, HALO_DEV), grad_out.reshape(DEVICES, NB_DEV, HID))

    def step_fn(carry, inputs):
        feats, degrees, nbr_idx, halo_idx, lengths, slot_rows, halo_degrees, upstream = inputs
        out_block, term_one, term_two, partial_value = device_block(weight_one, weight_two, feats, degrees, nbr_idx, halo_idx, lengths, halo_degrees, feat_table[slot_rows], emb_table[slot_rows], grad_table[slot_rows], upstream)
        return ((carry[0] + term_one, carry[1] + term_two), (out_block, partial_value))
    start = (jnp.zeros((FEAT, HID), jnp.float32), jnp.zeros((HID, HID), jnp.float32))
    sums, outputs = lax.scan(step_fn, start, blocks)
    out_embed = outputs[0].reshape(BATCH, HID)
    partials = outputs[1].reshape(HALO_TOTAL, HID)
    halo_grad = jnp.zeros((NODES, HID), jnp.float32).at[halo_rows].add(partials).astype(jnp.bfloat16)
    factor = 1.0 / jnp.sqrt(jnp.float32(BATCH))
    return (out_embed, halo_grad, sums[0] * factor, sums[1] * factor)
```

```python
import jax
import jax.numpy as jnp
from jax import lax
from jax.experimental import pallas as pl
from jax.experimental.pallas import tpu as pltpu
from jax.sharding import PartitionSpec as P

BF = jnp.bfloat16
F32 = jnp.float32
AXES = ("dp", "mp")
NB = 2048
NH = 512
HID = 512
FEAT = 128
STEP = 512
VMEM_LIMIT = 56 * 1024 * 1024


def dot(left, right):
    return jnp.dot(left, right, preferred_element_type=F32)


def dot_t(left, right):
    return lax.dot_general(left, right, (((1,), (1,)), ((), ())), preferred_element_type=F32)


def dot_tl(left, right):
    return lax.dot_general(left, right, (((0,), (0,)), ((), ())), preferred_element_type=F32)


def columns(row):
    n = row.shape[1]
    return jnp.concatenate(
        [jnp.broadcast_to(row[:, s : s + 128], (128, 128)).T for s in range(0, n, 128)], axis=0
    )


def scale_rows(x, col):
    reps = x.shape[1] // 128
    return x * (jnp.tile(col, (1, reps)) if reps > 1 else col)


def add_counts(dst_ref, row0, nbrs, width):
    rows = 16
    lane = lax.broadcasted_iota(jnp.int32, (rows, 128), 1)
    one = jnp.ones((rows, 128), BF)
    zero = jnp.zeros((rows, 128), BF)
    for r in range(0, nbrs.shape[0], rows):
        idx = [
            jnp.broadcast_to(nbrs[r : r + rows, k : k + 1], (rows, 128)).astype(jnp.int16)
            for k in range(8)
        ]
        for c in range(0, width, 128):
            here = (lane + c).astype(jnp.int16)
            acc = jnp.where(idx[0] == here, one, zero)
            for k in range(1, 8):
                acc = acc + jnp.where(idx[k] == here, one, zero)
            dst_ref[pl.ds(row0 + r, rows), c : c + 128] = acc


def halo_kernel(hn_ref, hl_ref, bdeg_ref, hdeg_ref, g_ref, h_ref, gt_ref, p_ref, lenb_ref):
    inv = lax.rsqrt(bdeg_ref[...].astype(F32))
    inv_h = lax.rsqrt(hdeg_ref[...].astype(F32))
    lenb_ref[...] = columns(hl_ref[...].astype(F32))

    def build(i, _):
        r = pl.multiple_of(i * 128, 128)
        nbrs = hn_ref[pl.ds(r, 128), :]
        slot = lax.broadcasted_iota(jnp.int32, nbrs.shape, 1).astype(F32)
        nbrs = jnp.where(slot < lenb_ref[pl.ds(r, 128), 0:8], nbrs, -1)
        add_counts(h_ref, r, nbrs, NH)
        return 0

    lax.fori_loop(0, NB // 128, build, 0)
    for s in range(0, NB, 512):
        gt = g_ref[s : s + 512, :].astype(F32).T * inv[:, s : s + 512]
        gt_ref[:, s : s + 512] = gt.astype(BF)
    pt = dot(gt_ref[...], h_ref[...]) * inv_h
    p_ref[...] = pt.T.astype(BF)


def halo_call(hn, hl, bdeg, hdeg, g):
    return pl.pallas_call(
        halo_kernel,
        out_shape=(
            jax.ShapeDtypeStruct((NB, NH), BF),
            jax.ShapeDtypeStruct((HID, NB), BF),
            jax.ShapeDtypeStruct((NH, HID), BF),
        ),
        scratch_shapes=[pltpu.VMEM((NB, 128), F32)],
        compiler_params=pltpu.CompilerParams(vmem_limit_bytes=VMEM_LIMIT),
        name="halo_part",
    )(hn, hl, bdeg, hdeg, g)


def pair_up(top, bottom):
    w = top.shape[1]
    t = top.reshape(64, 8, w)
    b = bottom.reshape(64, 8, w)
    low = lax.broadcasted_iota(jnp.int32, (64, 8, w), 1) < 4
    even = jnp.where(low, t, pltpu.roll(b, 4, 1))
    odd = jnp.where(low, pltpu.roll(t, 4, 1), b)
    return jnp.concatenate([even, odd], axis=1).astype(BF).reshape(1024, w)


def part_up(both):
    w = both.shape[1]
    x = both.reshape(64, 16, w).astype(F32)
    even, odd = x[:, 0:8], x[:, 8:16]
    low = lax.broadcasted_iota(jnp.int32, (64, 8, w), 1) < 4
    top = jnp.where(low, even, pltpu.roll(odd, 4, 1))
    bottom = jnp.where(low, pltpu.roll(even, 4, 1), odd)
    return top.reshape(512, w), bottom.reshape(512, w)


def pick_kernel(ask_ref, x_ref, e_ref, v_ref, p_ref, out_ref, s_ref):
    a = ask_ref[...]
    lane = lax.broadcasted_iota(jnp.int32, (64, 8, 8), 2)
    sub = lax.broadcasted_iota(jnp.int32, (64, 8, 8), 1)
    mine = jnp.where(lane == sub, jnp.broadcast_to(a[:, None, :], (64, 8, 8)), 0)
    col = jnp.sum(mine.astype(F32), axis=2, keepdims=True).reshape(512, 1).astype(jnp.int32)
    colb = jnp.broadcast_to(col, (512, 128))
    lanes = lax.broadcasted_iota(jnp.int32, (512, 128), 1)
    for c in range(0, 2048, 128):
        s_ref[:, c : c + 128] = jnp.where(colb == lanes + c, 1.0, 0.0).astype(BF)
    s = s_ref[...]
    out_ref[:, 0:512] = pair_up(dot(s, e_ref[...]), dot(s, v_ref[...]))
    p = p_ref[...].astype(F32)
    out_ref[:, 512:640] = pair_up(dot(s, x_ref[...]), p[:, 0:128])
    out_ref[:, 640:768] = pair_up(p[:, 128:256], p[:, 256:384])
    out_ref[:, 768:896] = pair_up(p[:, 384:512], p[:, 384:512])


def pick_call(asked, x, e, v, p):
    return pl.pallas_call(
        pick_kernel,
        out_shape=(
            jax.ShapeDtypeStruct((1024, 896), BF),
            jax.ShapeDtypeStruct((NH, NB), BF),
        ),
        compiler_params=pltpu.CompilerParams(vmem_limit_bytes=VMEM_LIMIT),
        name="pick_rows",
    )(asked, x, e, v, p)


def batch_kernel(nb_ref, bdeg_ref, f_ref, gt_ref, c_ref, cf_ref, st_ref, fs_ref):
    i = pl.program_id(0)

    @pl.when(i == 0)
    def _():
        col = columns(lax.rsqrt(bdeg_ref[...].astype(F32)))
        fs_ref[...] = (f_ref[...].astype(F32) * col).astype(BF)

    def build(t, _):
        r = pl.multiple_of(t * 64, 64)
        add_counts(c_ref, r, nb_ref[pl.ds(r, 64), :], NB)
        return 0

    lax.fori_loop(0, STEP // 64, build, 0)
    diag0 = pl.multiple_of(i * STEP, STEP)
    eye = (
        lax.broadcasted_iota(jnp.int32, (STEP, STEP), 0)
        == lax.broadcasted_iota(jnp.int32, (STEP, STEP), 1)
    ).astype(F32).astype(BF)
    c_ref[:, pl.ds(diag0, STEP)] = c_ref[:, pl.ds(diag0, STEP)] + eye
    c = c_ref[...]
    cf_ref[...] = dot(c, fs_ref[...])
    part = dot(gt_ref[...], c)

    @pl.when(i == 0)
    def _():
        st_ref[...] = part

    @pl.when(i > 0)
    def _():
        st_ref[...] = st_ref[...] + part


def batch_call(nb, bdeg, f, gt):
    return pl.pallas_call(
        batch_kernel,
        grid=(NB // STEP,),
        in_specs=[
            pl.BlockSpec((STEP, 8), lambda i: (i, 0)),
            pl.BlockSpec((1, NB), lambda i: (0, 0)),
            pl.BlockSpec((NB, FEAT), lambda i: (0, 0)),
            pl.BlockSpec((HID, STEP), lambda i: (0, i)),
        ],
        out_specs=[
            pl.BlockSpec((STEP, NB), lambda i: (i, 0)),
            pl.BlockSpec((STEP, FEAT), lambda i: (i, 0)),
            pl.BlockSpec((HID, NB), lambda i: (0, 0)),
        ],
        out_shape=(
            jax.ShapeDtypeStruct((NB, NB), BF),
            jax.ShapeDtypeStruct((NB, FEAT), F32),
            jax.ShapeDtypeStruct((HID, NB), F32),
        ),
        scratch_shapes=[pltpu.VMEM((NB, FEAT), BF)],
        compiler_params=pltpu.CompilerParams(vmem_limit_bytes=VMEM_LIMIT),
        name="batch_part",
    )(nb, bdeg, f, gt)


def main_kernel(
    r_ref, c_ref, h_ref, cf_ref, st_ref, gt_ref, w1_ref, w2_ref, bdeg_ref, hdeg_ref,
    u_ref, pa_ref, grads_ref,
    hid_ref, u1_ref, he_ref, hvt_ref, g1_ref, g2_ref, inv_ref,
):
    i = pl.program_id(0)
    inv = lax.rsqrt(bdeg_ref[...].astype(F32))

    @pl.when(i == 0)
    def _():
        col_h = columns(lax.rsqrt(hdeg_ref[...].astype(F32)))
        he, hv = part_up(r_ref[:, 0:512])
        he_ref[...] = scale_rows(he, col_h).astype(BF)
        hvt_ref[...] = scale_rows(hv, col_h).T.astype(BF)
        hx, p0 = part_up(r_ref[:, 512:640])
        hx = (hx * col_h).astype(BF)
        p1, p2 = part_up(r_ref[:, 640:768])
        p3, _ = part_up(r_ref[:, 768:896])
        pa_ref[:, 0:128] = p0.astype(BF)
        pa_ref[:, 128:256] = p1.astype(BF)
        pa_ref[:, 256:384] = p2.astype(BF)
        pa_ref[:, 384:512] = p3.astype(BF)
        inv_ref[...] = columns(inv)
        for s in range(0, NB, 512):
            col = inv_ref[s : s + 512, :]
            u1 = (cf_ref[s : s + 512, :] + dot(h_ref[s : s + 512, :], hx)).astype(BF)
            u1_ref[s : s + 512, :] = u1
            pre = scale_rows(dot(u1, w1_ref[...]), col)
            hid_ref[s : s + 512, :] = scale_rows(jax.nn.silu(pre), col).astype(BF)

    r = pl.multiple_of(i * STEP, STEP)
    h = h_ref[pl.ds(r, STEP), :]
    u = (dot(c_ref[...], hid_ref[...]) + dot(h, he_ref[...])).astype(BF)
    u_ref[...] = u
    g2 = dot(gt_ref[...], u)
    row = lax.rsqrt(bdeg_ref[:, pl.ds(r, STEP)].astype(F32))
    spread = ((st_ref[...] + dot_t(hvt_ref[...], h)) * row).astype(BF)
    back = dot(w2_ref[...], spread)
    u1 = u1_ref[pl.ds(r, STEP), :]
    w1t = w1_ref[...].astype(F32).T.astype(BF)
    pre = dot_t(w1t, u1) * row
    sig = jax.nn.sigmoid(pre)
    d_pre = (back * (sig * (1.0 + pre * (1.0 - sig))) * row).astype(BF)
    g1 = dot(d_pre, u1)

    @pl.when(i == 0)
    def _():
        g1_ref[...] = g1
        g2_ref[...] = g2

    @pl.when(i > 0)
    def _():
        g1_ref[...] += g1
        g2_ref[...] += g2

    @pl.when(i == pl.num_programs(0) - 1)
    def _():
        t1 = g1_ref[...].T.astype(BF)
        t2 = g2_ref[...].T.astype(BF)
        grads_ref[0:512, 0:256] = t2[:, 0:256]
        grads_ref[512:1024, 0:256] = t2[:, 256:512]
        for q in range(4):
            grads_ref[128 * q : 128 * q + 128, 256:384] = t1[:, 128 * q : 128 * q + 128]
        grads_ref[512:1024, 256:384] = jnp.zeros((512, 128), BF)


def main_call(recv, c, h, cf, st, gt, w1, w2, bdeg, hdeg):
    whole = lambda *shape: pl.BlockSpec(shape, lambda i: (0, 0))
    return pl.pallas_call(
        main_kernel,
        grid=(NB // STEP,),
        in_specs=[
            whole(1024, 896),
            pl.BlockSpec((STEP, NB), lambda i: (i, 0)),
            whole(NB, NH),
            whole(NB, FEAT),
            pl.BlockSpec((HID, STEP), lambda i: (0, i)),
            pl.BlockSpec((HID, STEP), lambda i: (0, i)),
            whole(FEAT, HID),
            whole(HID, HID),
            whole(1, NB),
            whole(1, NH),
        ],
        out_specs=[
            pl.BlockSpec((STEP, HID), lambda i: (i, 0)),
            whole(NH, HID),
            whole(1024, 384),
        ],
        out_shape=(
            jax.ShapeDtypeStruct((NB, HID), BF),
            jax.ShapeDtypeStruct((NH, HID), BF),
            jax.ShapeDtypeStruct((1024, 384), BF),
        ),
        scratch_shapes=[
            pltpu.VMEM((NB, HID), BF),
            pltpu.VMEM((NB, FEAT), BF),
            pltpu.VMEM((NH, HID), BF),
            pltpu.VMEM((HID, NH), BF),
            pltpu.VMEM((HID, FEAT), F32),
            pltpu.VMEM((HID, HID), F32),
            pltpu.VMEM((NB, 128), F32),
        ],
        compiler_params=pltpu.CompilerParams(vmem_limit_bytes=VMEM_LIMIT),
        name="main_part",
    )(recv, c, h, cf, st, gt, w1, w2, bdeg, hdeg)


def tail_kernel(u_ref, w2_ref, bdeg_ref, s_ref, pa_ref, out_ref, hg_ref):
    i = pl.program_id(0)
    r = pl.multiple_of(i * STEP, STEP)
    col = columns(lax.rsqrt(bdeg_ref[:, pl.ds(r, STEP)].astype(F32)))
    out_ref[...] = scale_rows(dot(u_ref[...], w2_ref[...]), col).astype(BF)
    hg_ref[...] = dot_tl(s_ref[...], pa_ref[...]).astype(BF)


def tail_call(u, w2, bdeg, s, pa):
    whole = lambda *shape: pl.BlockSpec(shape, lambda i: (0, 0))
    return pl.pallas_call(
        tail_kernel,
        grid=(NB // STEP,),
        in_specs=[
            pl.BlockSpec((STEP, HID), lambda i: (i, 0)),
            whole(HID, HID),
            whole(1, NB),
            pl.BlockSpec((NH, STEP), lambda i: (0, i)),
            whole(NH, HID),
        ],
        out_specs=[
            pl.BlockSpec((STEP, HID), lambda i: (i, 0)),
            pl.BlockSpec((STEP, HID), lambda i: (i, 0)),
        ],
        out_shape=(
            jax.ShapeDtypeStruct((NB, HID), BF),
            jax.ShapeDtypeStruct((NB, HID), BF),
        ),
        compiler_params=pltpu.CompilerParams(vmem_limit_bytes=VMEM_LIMIT),
        name="tail_part",
    )(u, w2, bdeg, s, pa)


def sum_kernel(x_ref, o_ref):
    total = jnp.sum(x_ref[...].astype(F32), axis=0)
    o_ref[...] = jnp.broadcast_to(total.astype(BF)[None], (128, 8, 384))


def sum_call(x):
    return pl.pallas_call(
        sum_kernel,
        out_shape=jax.ShapeDtypeStruct((128, 8, 384), BF),
        name="sum_part",
    )(x)


def final_kernel(x_ref, g1_ref, g2_ref):
    factor = 1.0 / 512.0
    g2_ref[:, 0:256] = x_ref[0:512, 0:256].astype(F32) * factor
    g2_ref[:, 256:512] = x_ref[512:1024, 0:256].astype(F32) * factor
    for q in range(4):
        part = x_ref[128 * q : 128 * q + 128, 256:384].astype(F32)
        g1_ref[:, 128 * q : 128 * q + 128] = part * factor


def final_call(x):
    return pl.pallas_call(
        final_kernel,
        out_shape=(
            jax.ShapeDtypeStruct((FEAT, HID), F32),
            jax.ShapeDtypeStruct((HID, HID), F32),
        ),
        name="final_part",
    )(x)


def exchange(x):
    return lax.all_to_all(x, AXES, split_axis=0, concat_axis=0, tiled=True)


def local(
    node_feats, batch_deg, batch_nbrs, halo_nbrs, halo_len, halo_rows, halo_deg,
    feat_table, emb_table, grad_table, weight_one, weight_two, grad_out,
):
    bdeg = batch_deg.reshape(1, NB)
    hdeg = halo_deg.reshape(1, NH)
    offsets = (halo_rows % NB).reshape(128, 1, 4)
    asked = exchange(offsets)
    h, gt, p = halo_call(halo_nbrs, halo_len.reshape(1, NB), bdeg, hdeg, grad_out)
    send, s = pick_call(asked.reshape(64, 8), feat_table, emb_table, grad_table, p)
    recv = exchange(send.reshape(128, 8, 896)).reshape(1024, 896)
    c, cf, st = batch_call(batch_nbrs, bdeg, node_feats, gt)
    u, pa, grads = main_call(recv, c, h, cf, st, gt, weight_one, weight_two, bdeg, hdeg)
    shares = exchange(grads.reshape(128, 8, 384))
    out_embed, halo_grad = tail_call(u, weight_two, bdeg, s, pa)
    sums = exchange(sum_call(shares)).reshape(1024, 384)
    grad_one, grad_two = final_call(sums)
    return out_embed, halo_grad, grad_one, grad_two


def solution(mesh):
    rows = P(AXES, None)
    flat = P(AXES)
    return jax.shard_map(
        local,
        mesh=mesh,
        in_specs=(
            rows, flat, rows, rows, flat, flat, flat, rows, rows, rows, P(), P(), rows,
        ),
        out_specs=(rows, rows, P(), P()),
        check_vma=False,
    )
```

```python
import jax
import jax.numpy as jnp
from jax import lax
from jax.experimental import pallas as pl
from jax.experimental.pallas import tpu as pltpu
from jax.sharding import PartitionSpec as P

BF = jnp.bfloat16
F32 = jnp.float32
AXES = ("dp", "mp")
NB = 2048
NH = 512
HID = 512
FEAT = 128
STEP = 512
VMEM_LIMIT = 56 * 1024 * 1024


def dot(left, right):
    return jnp.dot(left, right, preferred_element_type=F32)


def dot_t(left, right):
    return lax.dot_general(left, right, (((1,), (1,)), ((), ())), preferred_element_type=F32)


def dot_tl(left, right):
    return lax.dot_general(left, right, (((0,), (0,)), ((), ())), preferred_element_type=F32)


def columns(row):
    n = row.shape[1]
    return jnp.concatenate(
        [jnp.broadcast_to(row[:, s : s + 128], (128, 128)).T for s in range(0, n, 128)], axis=0
    )


def scale_rows(x, col):
    reps = x.shape[1] // 128
    return x * (jnp.tile(col, (1, reps)) if reps > 1 else col)


def count_tiles(dst_ref, nbrs, rows0, n_rows):
    times = jnp.ones(nbrs.shape, jnp.int32)
    for k in range(1, 8):
        times = times + (nbrs == pltpu.roll(nbrs, k, 0)).astype(jnp.int32)
    times = times.astype(F32)
    zero = jnp.zeros((16, 128), BF)
    sub = lax.broadcasted_iota(jnp.int32, (16, 128), 0)
    for c in range(0, nbrs.shape[1], 128):
        idx = [
            jnp.broadcast_to(nbrs[k : k + 1, c : c + 128], (16, 128)).astype(jnp.int16)
            for k in range(8)
        ]
        val = [jnp.broadcast_to(times[k : k + 1, c : c + 128], (16, 128)).astype(BF) for k in range(8)]

        def group(t, _):
            base = pl.multiple_of(t * 128, 128)
            first = (sub + (base + rows0)).astype(jnp.int16)
            for r in range(0, 128, 16):
                here = first + jnp.int16(r)
                acc = zero
                for k in range(8):
                    acc = jnp.where(idx[k] == here, val[k], acc)
                dst_ref[pl.ds(base + r, 16), c : c + 128] = acc
            return 0

        lax.fori_loop(0, n_rows // 128, group, 0)


def halo_kernel(hn_ref, hl_ref, bdeg_ref, hdeg_ref, g_hbm, h_ref, gs_ref, p_ref, g_ref, sem):
    copy = pltpu.make_async_copy(g_hbm, g_ref, sem)
    copy.start()
    nbrs = hn_ref[...]
    slot = lax.broadcasted_iota(jnp.int32, nbrs.shape, 0)
    nbrs = jnp.where(slot < hl_ref[...], nbrs, -1)
    count_tiles(h_ref, nbrs, 0, NH)
    inv = columns(lax.rsqrt(bdeg_ref[...].astype(F32)))
    inv_h = columns(lax.rsqrt(hdeg_ref[...].astype(F32)))
    copy.wait()
    for s in range(0, NB, 512):
        gs_ref[s : s + 512, :] = scale_rows(g_ref[s : s + 512, :].astype(F32), inv[s : s + 512]).astype(BF)
    p_ref[...] = scale_rows(dot(h_ref[...], gs_ref[...]), inv_h).astype(BF)


def any_spec():
    return pl.BlockSpec(memory_space=pl.ANY)


def vmem_spec():
    return pl.BlockSpec(memory_space=pltpu.VMEM)


def halo_call(hn, hl, bdeg, hdeg, g):
    return pl.pallas_call(
        halo_kernel,
        in_specs=[vmem_spec()] * 4 + [any_spec()],
        out_specs=[vmem_spec()] * 3,
        out_shape=(
            jax.ShapeDtypeStruct((NH, NB), BF),
            jax.ShapeDtypeStruct((NB, HID), BF),
            jax.ShapeDtypeStruct((NH, HID), BF),
        ),
        scratch_shapes=[pltpu.VMEM((NB, HID), BF), pltpu.SemaphoreType.DMA(())],
        compiler_params=pltpu.CompilerParams(vmem_limit_bytes=VMEM_LIMIT),
        name="halo_part",
    )(hn, hl, bdeg, hdeg, g)


def pair_up(top, bottom):
    w = top.shape[1]
    t = top.reshape(64, 8, w)
    b = bottom.reshape(64, 8, w)
    low = lax.broadcasted_iota(jnp.int32, (64, 8, w), 1) < 4
    even = jnp.where(low, t, pltpu.roll(b, 4, 1))
    odd = jnp.where(low, pltpu.roll(t, 4, 1), b)
    return jnp.concatenate([even, odd], axis=1).astype(BF).reshape(1024, w)


def part_up(both):
    w = both.shape[1]
    x = both.reshape(64, 16, w).astype(F32)
    even, odd = x[:, 0:8], x[:, 8:16]
    low = lax.broadcasted_iota(jnp.int32, (64, 8, w), 1) < 4
    top = jnp.where(low, even, pltpu.roll(odd, 4, 1))
    bottom = jnp.where(low, pltpu.roll(even, 4, 1), odd)
    return top.reshape(512, w), bottom.reshape(512, w)


def pick_kernel(ask_ref, x_hbm, e_hbm, v_hbm, p_ref, out_ref, s_ref, x_ref, e_ref, v_ref, sems):
    copies = [
        pltpu.make_async_copy(src, dst, sems.at[n])
        for n, (src, dst) in enumerate(((e_hbm, e_ref), (v_hbm, v_ref), (x_hbm, x_ref)))
    ]
    for copy in copies:
        copy.start()
    a = ask_ref[...].reshape(64, 2, 1, 4)
    sub = lax.broadcasted_iota(jnp.int32, (64, 8, 4), 1)
    lane = lax.broadcasted_iota(jnp.int32, (64, 8, 4), 2)
    mine = jnp.where(
        sub < 4, jnp.broadcast_to(a[:, 0], (64, 8, 4)), jnp.broadcast_to(a[:, 1], (64, 8, 4))
    )
    mine = jnp.where(lane == (sub & 3), mine & (NB - 1), 0)
    col = jnp.sum(mine.astype(F32), axis=2, keepdims=True).reshape(512, 1).astype(jnp.int32)
    colb = jnp.broadcast_to(col, (512, 128)).astype(jnp.int16)
    lanes = lax.broadcasted_iota(jnp.int32, (512, 128), 1)
    one = jnp.ones((512, 128), BF)
    for c in range(0, NB, 128):
        s_ref[:, c : c + 128] = jnp.where(colb == (lanes + c).astype(jnp.int16), one, one - one)
    p = p_ref[...].astype(F32)
    out_ref[:, 640:768] = pair_up(p[:, 128:256], p[:, 256:384])
    out_ref[:, 768:896] = pair_up(p[:, 384:512], p[:, 384:512])
    s = s_ref[...]
    copies[0].wait()
    picked = dot(s, e_ref[...])
    copies[1].wait()
    out_ref[:, 0:512] = pair_up(picked, dot(s, v_ref[...]))
    copies[2].wait()
    out_ref[:, 512:640] = pair_up(dot(s, x_ref[...]), p[:, 0:128])


def pick_call(asked, x, e, v, p):
    return pl.pallas_call(
        pick_kernel,
        in_specs=[vmem_spec(), any_spec(), any_spec(), any_spec(), vmem_spec()],
        out_specs=[vmem_spec()] * 2,
        out_shape=(
            jax.ShapeDtypeStruct((1024, 896), BF),
            jax.ShapeDtypeStruct((NH, NB), BF),
        ),
        scratch_shapes=[
            pltpu.VMEM((NB, FEAT), BF),
            pltpu.VMEM((NB, HID), BF),
            pltpu.VMEM((NB, HID), BF),
            pltpu.SemaphoreType.DMA((3,)),
        ],
        compiler_params=pltpu.CompilerParams(vmem_limit_bytes=VMEM_LIMIT),
        name="pick_rows",
    )(asked, x, e, v, p)


def batch_kernel(nb_ref, bdeg_ref, f_ref, gs_ref, c_ref, cf_ref, sp_ref, fs_ref):
    i = pl.program_id(0)

    @pl.when(i == 0)
    def _():
        col = columns(lax.rsqrt(bdeg_ref[...].astype(F32)))
        fs_ref[...] = (f_ref[...].astype(F32) * col).astype(BF)

    r0 = pl.multiple_of(i * STEP, STEP)
    count_tiles(c_ref, nb_ref[...], r0, STEP)
    eye = (
        lax.broadcasted_iota(jnp.int32, (128, 128), 0)
        == lax.broadcasted_iota(jnp.int32, (128, 128), 1)
    ).astype(F32).astype(BF)
    for r in range(0, STEP, 128):
        at = pl.ds(pl.multiple_of(r0 + r, 128), 128)
        c_ref[r : r + 128, at] = c_ref[r : r + 128, at] + eye
    c = c_ref[...]
    sp_ref[...] = dot(c, gs_ref[...])
    part = dot_tl(c, fs_ref[pl.ds(r0, STEP), :])

    @pl.when(i == 0)
    def _():
        cf_ref[...] = part

    @pl.when(i > 0)
    def _():
        cf_ref[...] += part


def batch_call(nb, bdeg, f, gs):
    whole = lambda *shape: pl.BlockSpec(shape, lambda i: (0, 0))
    return pl.pallas_call(
        batch_kernel,
        grid=(NB // STEP,),
        in_specs=[whole(8, NB), whole(1, NB), whole(NB, FEAT), whole(NB, HID)],
        out_specs=[
            pl.BlockSpec((STEP, NB), lambda i: (i, 0)),
            whole(NB, FEAT),
            pl.BlockSpec((STEP, HID), lambda i: (i, 0)),
        ],
        out_shape=(
            jax.ShapeDtypeStruct((NB, NB), BF),
            jax.ShapeDtypeStruct((NB, FEAT), F32),
            jax.ShapeDtypeStruct((NB, HID), F32),
        ),
        scratch_shapes=[pltpu.VMEM((NB, FEAT), BF)],
        compiler_params=pltpu.CompilerParams(vmem_limit_bytes=VMEM_LIMIT),
        name="batch_part",
    )(nb, bdeg, f, gs)


def main_kernel(
    r_hbm, h_hbm, cf_hbm, c_hbm, sp_hbm, gs_hbm, w1_ref, w2_ref, bdeg_ref, hdeg_ref,
    u_ref, pa_ref, grads_ref,
    r_ref, h_ref, cf_ref, c_ref, sp_ref, gs_ref,
    hid_ref, der_ref, u1_ref, he_ref, hv_ref, g1_ref, g2_ref, sems,
):
    pairs = (
        (r_hbm, r_ref), (h_hbm, h_ref), (cf_hbm, cf_ref), (c_hbm, c_ref), (gs_hbm, gs_ref), (sp_hbm, sp_ref),
    )
    copies = [pltpu.make_async_copy(src, dst, sems.at[n]) for n, (src, dst) in enumerate(pairs)]
    for copy in copies:
        copy.start()
    inv = columns(lax.rsqrt(bdeg_ref[...].astype(F32)))
    col_h = columns(lax.rsqrt(hdeg_ref[...].astype(F32)))
    copies[0].wait()
    hx, p0 = part_up(r_ref[:, 512:640])
    hx = (hx * col_h).astype(BF)
    copies[1].wait()
    copies[2].wait()
    for s in range(0, NB, STEP):
        col = inv[s : s + STEP]
        u1 = (cf_ref[s : s + STEP, :] + dot_tl(h_ref[:, s : s + STEP], hx)).astype(BF)
        u1_ref[s : s + STEP, :] = u1
        pre = scale_rows(dot(u1, w1_ref[...]), col)
        sig = 0.5 + 0.5 * jnp.tanh(0.5 * pre)
        hid_ref[s : s + STEP, :] = scale_rows(pre * sig, col).astype(BF)
        der_ref[s : s + STEP, :] = scale_rows(sig * (1.0 + pre * (1.0 - sig)), col * col)
    he, hv = part_up(r_ref[:, 0:512])
    he_ref[...] = scale_rows(he, col_h).astype(BF)
    hv_ref[...] = scale_rows(hv, col_h).astype(BF)
    p1, p2 = part_up(r_ref[:, 640:768])
    p3, _ = part_up(r_ref[:, 768:896])
    pa_ref[:, 0:128] = p0.astype(BF)
    pa_ref[:, 128:256] = p1.astype(BF)
    pa_ref[:, 256:384] = p2.astype(BF)
    pa_ref[:, 384:512] = p3.astype(BF)
    for copy in copies[3:]:
        copy.wait()
    for s in range(0, NB, STEP):
        h = h_ref[:, s : s + STEP]
        u = (dot_tl(c_ref[:, s : s + STEP], hid_ref[...]) + dot_tl(h, he_ref[...])).astype(BF)
        u_ref[s : s + STEP, :] = u
        spread = (sp_ref[s : s + STEP, :] + dot_tl(h, hv_ref[...])).astype(BF)
        d_pre = (dot_t(spread, w2_ref[...]) * der_ref[s : s + STEP, :]).astype(BF)
        g2 = dot_tl(u, gs_ref[s : s + STEP, :])
        g1 = dot_tl(u1_ref[s : s + STEP, :], d_pre)
        if s == 0:
            g1_ref[...] = g1
            g2_ref[...] = g2
        else:
            g1_ref[...] += g1
            g2_ref[...] += g2
    grads_ref[0:512, 0:256] = g2_ref[:, 0:256].astype(BF)
    grads_ref[512:1024, 0:256] = g2_ref[:, 256:512].astype(BF)
    for q in range(4):
        grads_ref[128 * q : 128 * q + 128, 256:384] = g1_ref[:, 128 * q : 128 * q + 128].astype(BF)
    grads_ref[512:1024, 256:384] = jnp.zeros((512, 128), BF)


def main_call(recv, c, h, cf, sp, gs, w1, w2, bdeg, hdeg):
    return pl.pallas_call(
        main_kernel,
        in_specs=[any_spec()] * 6 + [vmem_spec()] * 4,
        out_specs=[vmem_spec()] * 3,
        out_shape=(
            jax.ShapeDtypeStruct((NB, HID), BF),
            jax.ShapeDtypeStruct((NH, HID), BF),
            jax.ShapeDtypeStruct((1024, 384), BF),
        ),
        scratch_shapes=[
            pltpu.VMEM((1024, 896), BF),
            pltpu.VMEM((NH, NB), BF),
            pltpu.VMEM((NB, FEAT), F32),
            pltpu.VMEM((NB, NB), BF),
            pltpu.VMEM((NB, HID), F32),
            pltpu.VMEM((NB, HID), BF),
            pltpu.VMEM((NB, HID), BF),
            pltpu.VMEM((NB, HID), F32),
            pltpu.VMEM((NB, FEAT), BF),
            pltpu.VMEM((NH, HID), BF),
            pltpu.VMEM((NH, HID), BF),
            pltpu.VMEM((FEAT, HID), F32),
            pltpu.VMEM((HID, HID), F32),
            pltpu.SemaphoreType.DMA((6,)),
        ],
        compiler_params=pltpu.CompilerParams(vmem_limit_bytes=VMEM_LIMIT),
        name="main_part",
    )(recv, h, cf, c, sp, gs, w1, w2, bdeg, hdeg)


def tail_kernel(u_ref, w2_ref, bdeg_ref, s_ref, pa_ref, out_ref, hg_ref):
    i = pl.program_id(0)
    r = pl.multiple_of(i * STEP, STEP)
    col = columns(lax.rsqrt(bdeg_ref[:, pl.ds(r, STEP)].astype(F32)))
    out_ref[...] = scale_rows(dot(u_ref[...], w2_ref[...]), col).astype(BF)
    hg_ref[...] = dot_tl(s_ref[...], pa_ref[...]).astype(BF)


def tail_call(u, w2, bdeg, s, pa):
    whole = lambda *shape: pl.BlockSpec(shape, lambda i: (0, 0))
    return pl.pallas_call(
        tail_kernel,
        grid=(NB // STEP,),
        in_specs=[
            pl.BlockSpec((STEP, HID), lambda i: (i, 0)),
            whole(HID, HID),
            whole(1, NB),
            pl.BlockSpec((NH, STEP), lambda i: (0, i)),
            whole(NH, HID),
        ],
        out_specs=[
            pl.BlockSpec((STEP, HID), lambda i: (i, 0)),
            pl.BlockSpec((STEP, HID), lambda i: (i, 0)),
        ],
        out_shape=(
            jax.ShapeDtypeStruct((NB, HID), BF),
            jax.ShapeDtypeStruct((NB, HID), BF),
        ),
        compiler_params=pltpu.CompilerParams(vmem_limit_bytes=VMEM_LIMIT),
        name="tail_part",
    )(u, w2, bdeg, s, pa)


def sum_kernel(x_ref, o_ref):
    total = jnp.sum(x_ref[...].astype(F32), axis=0)
    o_ref[...] = jnp.broadcast_to(total.astype(BF)[None], (128, 8, 384))


def sum_call(x):
    return pl.pallas_call(
        sum_kernel,
        out_shape=jax.ShapeDtypeStruct((128, 8, 384), BF),
        name="sum_part",
    )(x)


def final_kernel(x_ref, g1_ref, g2_ref):
    factor = 1.0 / 512.0
    g2_ref[:, 0:256] = x_ref[0:512, 0:256].astype(F32) * factor
    g2_ref[:, 256:512] = x_ref[512:1024, 0:256].astype(F32) * factor
    for q in range(4):
        part = x_ref[128 * q : 128 * q + 128, 256:384].astype(F32)
        g1_ref[:, 128 * q : 128 * q + 128] = part * factor


def final_call(x):
    return pl.pallas_call(
        final_kernel,
        out_shape=(
            jax.ShapeDtypeStruct((FEAT, HID), F32),
            jax.ShapeDtypeStruct((HID, HID), F32),
        ),
        name="final_part",
    )(x)


def exchange(x):
    return lax.all_to_all(x, AXES, split_axis=0, concat_axis=0, tiled=True)


def local(
    node_feats, batch_deg, batch_nbrs, halo_nbrs, halo_len, halo_rows, halo_deg,
    feat_table, emb_table, grad_table, weight_one, weight_two, grad_out,
):
    bdeg = batch_deg.reshape(1, NB)
    hdeg = halo_deg.reshape(1, NH)
    asked = exchange(halo_rows.reshape(128, 1, 4))
    h, gs, p = halo_call(halo_nbrs.T, halo_len.reshape(1, NB), bdeg, hdeg, grad_out)
    send, s = pick_call(asked, feat_table, emb_table, grad_table, p)
    recv = exchange(send.reshape(128, 8, 896)).reshape(1024, 896)
    c, cf, sp = batch_call(batch_nbrs.T, bdeg, node_feats, gs)
    u, pa, grads = main_call(recv, c, h, cf, sp, gs, weight_one, weight_two, bdeg, hdeg)
    shares = exchange(grads.reshape(128, 8, 384))
    out_embed, halo_grad = tail_call(u, weight_two, bdeg, s, pa)
    sums = exchange(sum_call(shares)).reshape(1024, 384)
    grad_one, grad_two = final_call(sums)
    return out_embed, halo_grad, grad_one, grad_two


def solution(mesh):
    rows = P(AXES, None)
    flat = P(AXES)
    return jax.shard_map(
        local,
        mesh=mesh,
        in_specs=(
            rows, flat, rows, rows, flat, flat, flat, rows, rows, rows, P(), P(), rows,
        ),
        out_specs=(rows, rows, P(), P()),
        check_vma=False,
    )
```

```python
import jax
import jax.numpy as jnp
from jax import lax
from jax.experimental import pallas as pl
from jax.experimental.pallas import tpu as pltpu
from jax.sharding import PartitionSpec as P

BF = jnp.bfloat16
F32 = jnp.float32
AXES = ("dp", "mp")
NB = 2048
NH = 512
HID = 512
FEAT = 128
STEP = 512


def hbm_spec():
    return pl.BlockSpec(memory_space=pltpu.HBM)


def vmem_spec():
    return pl.BlockSpec(memory_space=pltpu.VMEM)


def held(*shape, dtype=BF):
    return pltpu.VMEM(shape, dtype)


def keep(x):
    return pltpu.with_memory_space_constraint(x, pltpu.VMEM)


def leave(x):
    return pltpu.with_memory_space_constraint(x, pltpu.HBM)


def limit(mib):
    return pltpu.CompilerParams(vmem_limit_bytes=mib * 1024 * 1024)


def dot(left, right):
    return jnp.dot(left, right, preferred_element_type=F32)


def dot_t(left, right):
    return lax.dot_general(left, right, (((1,), (1,)), ((), ())), preferred_element_type=F32)


def dot_tl(left, right):
    return lax.dot_general(left, right, (((0,), (0,)), ((), ())), preferred_element_type=F32)


def columns(row):
    n = row.shape[1]
    return jnp.concatenate(
        [jnp.broadcast_to(row[:, s : s + 128], (128, 128)).T for s in range(0, n, 128)], axis=0
    )


def scale_rows(x, col):
    reps = x.shape[1] // 128
    return x * (jnp.tile(col, (1, reps)) if reps > 1 else col)


def count_tiles(dst_ref, nbrs, rows0, n_rows):
    times = jnp.ones(nbrs.shape, jnp.int32)
    for k in range(1, 8):
        times = times + (nbrs == pltpu.roll(nbrs, k, 0)).astype(jnp.int32)
    times = times.astype(F32)
    zero = jnp.zeros((16, 128), BF)
    sub = lax.broadcasted_iota(jnp.int32, (16, 128), 0)
    for c in range(0, nbrs.shape[1], 128):
        idx = [
            jnp.broadcast_to(nbrs[k : k + 1, c : c + 128], (16, 128)).astype(jnp.int16)
            for k in range(8)
        ]
        val = [jnp.broadcast_to(times[k : k + 1, c : c + 128], (16, 128)).astype(BF) for k in range(8)]

        def group(t, _):
            base = pl.multiple_of(t * 128, 128)
            first = (sub + (base + rows0)).astype(jnp.int16)
            for r in range(0, 128, 16):
                here = first + jnp.int16(r)
                acc = zero
                for k in range(8):
                    acc = jnp.where(idx[k] == here, val[k], acc)
                dst_ref[pl.ds(base + r, 16), c : c + 128] = acc
            return 0

        lax.fori_loop(0, n_rows // 128, group, 0)


def halo_kernel(
    hn_ref, hl_ref, bdeg_ref, hdeg_ref, g_hbm, h_hbm, gs_hbm, p_ref, g_ref, h_ref, gs_ref, sems
):
    copy_in = pltpu.make_async_copy(g_hbm, g_ref, sems.at[0])
    copy_in.start()
    nbrs = hn_ref[...]
    slot = lax.broadcasted_iota(jnp.int32, nbrs.shape, 0)
    nbrs = jnp.where(slot < hl_ref[...], nbrs, -1)
    count_tiles(h_ref, nbrs, 0, NH)
    copy_h = pltpu.make_async_copy(h_ref, h_hbm, sems.at[1])
    copy_h.start()
    inv = columns(lax.rsqrt(bdeg_ref[...].astype(F32)))
    inv_h = columns(lax.rsqrt(hdeg_ref[...].astype(F32)))
    copy_in.wait()
    for s in range(0, NB, STEP):
        gs = scale_rows(g_ref[s : s + STEP, :].astype(F32), inv[s : s + STEP])
        gs_ref[s : s + STEP, :] = gs.astype(BF)
    copy_gs = pltpu.make_async_copy(gs_ref, gs_hbm, sems.at[2])
    copy_gs.start()
    p_ref[...] = scale_rows(dot(h_ref[...], gs_ref[...]), inv_h).astype(BF)
    copy_h.wait()
    copy_gs.wait()


def halo_call(hn, hl, bdeg, hdeg, g):
    return pl.pallas_call(
        halo_kernel,
        in_specs=[vmem_spec()] * 4 + [hbm_spec()],
        out_specs=[hbm_spec(), hbm_spec(), vmem_spec()],
        out_shape=(
            pltpu.HBM((NH, NB), BF),
            pltpu.HBM((NB, HID), BF),
            held(NH, HID),
        ),
        scratch_shapes=[
            pltpu.VMEM((NB, HID), BF),
            pltpu.VMEM((NH, NB), BF),
            pltpu.VMEM((NB, HID), BF),
            pltpu.SemaphoreType.DMA((3,)),
        ],
        compiler_params=limit(58),
        name="halo_part",
    )(hn, hl, bdeg, hdeg, leave(g))


def pair_up(top, bottom):
    w = top.shape[1]
    t = top.reshape(64, 8, w)
    b = bottom.reshape(64, 8, w)
    low = lax.broadcasted_iota(jnp.int32, (64, 8, w), 1) < 4
    even = jnp.where(low, t, pltpu.roll(b, 4, 1))
    odd = jnp.where(low, pltpu.roll(t, 4, 1), b)
    return jnp.concatenate([even, odd], axis=1).astype(BF).reshape(1024, w)


def part_up(both):
    w = both.shape[1]
    x = both.reshape(64, 16, w).astype(F32)
    even, odd = x[:, 0:8], x[:, 8:16]
    low = lax.broadcasted_iota(jnp.int32, (64, 8, w), 1) < 4
    top = jnp.where(low, even, pltpu.roll(odd, 4, 1))
    bottom = jnp.where(low, pltpu.roll(even, 4, 1), odd)
    return top.reshape(512, w), bottom.reshape(512, w)


def selector(ask_ref, s_ref):
    a = ask_ref[...].reshape(64, 2, 1, 4)
    sub = lax.broadcasted_iota(jnp.int32, (64, 8, 4), 1)
    lane = lax.broadcasted_iota(jnp.int32, (64, 8, 4), 2)
    mine = jnp.where(
        sub < 4, jnp.broadcast_to(a[:, 0], (64, 8, 4)), jnp.broadcast_to(a[:, 1], (64, 8, 4))
    )
    mine = jnp.where(lane == (sub & 3), mine & (NB - 1), 0)
    col = jnp.sum(mine.astype(F32), axis=2, keepdims=True).reshape(512, 1).astype(jnp.int32)
    colb = jnp.broadcast_to(col, (512, 128))
    lanes = lax.broadcasted_iota(jnp.int32, (512, 128), 1)
    for c in range(0, NB, 128):
        s_ref[:, c : c + 128] = jnp.where(colb == lanes + c, 1.0, 0.0).astype(BF)


def pick_kernel(
    ask_ref, x_hbm, e_hbm, v_hbm, p_ref, out_hbm, s_ref, x_ref, e_ref, v_ref, out_ref, sems
):
    copies = [
        pltpu.make_async_copy(src, dst, sems.at[n])
        for n, (src, dst) in enumerate(((e_hbm, e_ref), (v_hbm, v_ref), (x_hbm, x_ref)))
    ]
    for copy in copies:
        copy.start()
    selector(ask_ref, s_ref)
    s = s_ref[...]
    copies[0].wait()
    picked = dot(s, e_ref[...])
    copies[1].wait()
    out_ref[:, 0:512] = pair_up(picked, dot(s, v_ref[...]))
    left = pltpu.make_async_copy(out_ref.at[:, 0:512], out_hbm.at[:, 0:512], sems.at[3])
    left.start()
    copies[2].wait()
    p = p_ref[...].astype(F32)
    out_ref[:, 512:640] = pair_up(dot(s, x_ref[...]), p[:, 0:128])
    out_ref[:, 640:768] = pair_up(p[:, 128:256], p[:, 256:384])
    out_ref[:, 768:896] = pair_up(p[:, 384:512], p[:, 384:512])
    right = pltpu.make_async_copy(out_ref.at[:, 512:896], out_hbm.at[:, 512:896], sems.at[4])
    right.start()
    left.wait()
    right.wait()


def pick_call(asked, x, e, v, p):
    return pl.pallas_call(
        pick_kernel,
        in_specs=[vmem_spec(), hbm_spec(), hbm_spec(), hbm_spec(), vmem_spec()],
        out_specs=hbm_spec(),
        out_shape=pltpu.HBM((1024, 896), BF),
        scratch_shapes=[
            pltpu.VMEM((NH, NB), BF),
            pltpu.VMEM((NB, FEAT), BF),
            pltpu.VMEM((NB, HID), BF),
            pltpu.VMEM((NB, HID), BF),
            pltpu.VMEM((1024, 896), BF),
            pltpu.SemaphoreType.DMA((5,)),
        ],
        compiler_params=limit(58),
        name="pick_rows",
    )(keep(asked), leave(x), leave(e), leave(v), keep(p))


def batch_kernel(
    nb_ref, bdeg_ref, f_ref, gs_ref, c_hbm, cf_ref, sp_hbm, fs_ref, c_ref, sp_ref, sems
):
    col = columns(lax.rsqrt(bdeg_ref[...].astype(F32)))
    fs_ref[...] = (f_ref[...].astype(F32) * col).astype(BF)
    eye = (
        lax.broadcasted_iota(jnp.int32, (128, 128), 0)
        == lax.broadcasted_iota(jnp.int32, (128, 128), 1)
    ).astype(F32).astype(BF)
    count_tiles(c_ref, nb_ref[...], 0, NB)
    for r in range(0, NB, 128):
        c_ref[r : r + 128, r : r + 128] = c_ref[r : r + 128, r : r + 128] + eye
    copies = [pltpu.make_async_copy(c_ref, c_hbm, sems.at[0])]
    copies[0].start()
    for n, r in enumerate(range(0, NB, STEP)):
        at = slice(r, r + STEP)
        sp_ref[at, :] = dot(c_ref[at, :], gs_ref[...])
        copies.append(pltpu.make_async_copy(sp_ref.at[at], sp_hbm.at[at], sems.at[1 + n]))
        copies[-1].start()
        cf_ref[at, :] = dot_tl(c_ref[:, at], fs_ref[...])
    for copy in copies:
        copy.wait()


def batch_call(nb, bdeg, f, gs):
    return pl.pallas_call(
        batch_kernel,
        in_specs=[vmem_spec()] * 4,
        out_specs=[hbm_spec(), vmem_spec(), hbm_spec()],
        out_shape=(
            pltpu.HBM((NB, NB), BF),
            pltpu.HBM((NB, FEAT), F32),
            pltpu.HBM((NB, HID), F32),
        ),
        scratch_shapes=[
            pltpu.VMEM((NB, FEAT), BF),
            pltpu.VMEM((NB, NB), BF),
            pltpu.VMEM((NB, HID), F32),
            pltpu.SemaphoreType.DMA((5,)),
        ],
        compiler_params=limit(58),
        name="batch_part",
    )(nb, bdeg, f, gs)


def main_kernel(
    r_ref, h_hbm, cf_hbm, c_hbm, sp_hbm, gs_hbm, w1_ref, w2_ref, bdeg_ref, hdeg_ref,
    u_hbm, pa_ref, grads_ref,
    h_ref, cf_ref, c_ref, sp_ref, gs_ref, u_ref,
    hid_ref, der_ref, u1_ref, he_ref, hv_ref, g1_ref, g2_ref, sems,
):
    pairs = (
        (h_hbm, h_ref), (cf_hbm, cf_ref), (c_hbm, c_ref), (gs_hbm, gs_ref), (sp_hbm, sp_ref),
    )
    copies = [pltpu.make_async_copy(src, dst, sems.at[n]) for n, (src, dst) in enumerate(pairs)]
    for copy in copies[:2]:
        copy.start()
    inv = columns(lax.rsqrt(bdeg_ref[...].astype(F32)))
    col_h = columns(lax.rsqrt(hdeg_ref[...].astype(F32)))
    for copy in copies[:2]:
        copy.wait()
    for copy in copies[2:]:
        copy.start()
    hx, p0 = part_up(r_ref[:, 512:640])
    hx = (hx * col_h).astype(BF)
    for s in range(0, NB, STEP):
        col = inv[s : s + STEP]
        u1 = (cf_ref[s : s + STEP, :] + dot_tl(h_ref[:, s : s + STEP], hx)).astype(BF)
        u1_ref[s : s + STEP, :] = u1
        pre = scale_rows(dot(u1, w1_ref[...]), col)
        sig = 0.5 + 0.5 * jnp.tanh(0.5 * pre)
        hid_ref[s : s + STEP, :] = scale_rows(pre * sig, col).astype(BF)
        der_ref[s : s + STEP, :] = scale_rows(sig * (1.0 + pre * (1.0 - sig)), col * col)
    he, hv = part_up(r_ref[:, 0:512])
    he_ref[...] = scale_rows(he, col_h).astype(BF)
    hv_ref[...] = scale_rows(hv, col_h).astype(BF)
    p1, p2 = part_up(r_ref[:, 640:768])
    p3, _ = part_up(r_ref[:, 768:896])
    pa_ref[:, 0:128] = p0.astype(BF)
    pa_ref[:, 128:256] = p1.astype(BF)
    pa_ref[:, 256:384] = p2.astype(BF)
    pa_ref[:, 384:512] = p3.astype(BF)
    for copy in copies[2:]:
        copy.wait()
    outs = []
    for s in range(0, NB, STEP):
        h = h_ref[:, s : s + STEP]
        u = (dot_tl(c_ref[:, s : s + STEP], hid_ref[...]) + dot_tl(h, he_ref[...])).astype(BF)
        at = slice(s, s + STEP)
        u_ref[at, :] = u
        outs.append(pltpu.make_async_copy(u_ref.at[at], u_hbm.at[at], sems.at[5 + s // STEP]))
        outs[-1].start()
        spread = (sp_ref[s : s + STEP, :] + dot_tl(h, hv_ref[...])).astype(BF)
        d_pre = (dot_t(spread, w2_ref[...]) * der_ref[s : s + STEP, :]).astype(BF)
        g2 = dot_tl(u, gs_ref[s : s + STEP, :])
        g1 = dot_tl(u1_ref[s : s + STEP, :], d_pre)
        if s == 0:
            g1_ref[...] = g1
            g2_ref[...] = g2
        else:
            g1_ref[...] += g1
            g2_ref[...] += g2
    grads_ref[0:512, 0:256] = g2_ref[:, 0:256].astype(BF)
    grads_ref[512:1024, 0:256] = g2_ref[:, 256:512].astype(BF)
    for q in range(4):
        grads_ref[128 * q : 128 * q + 128, 256:384] = g1_ref[:, 128 * q : 128 * q + 128].astype(BF)
    grads_ref[512:1024, 256:384] = jnp.zeros((512, 128), BF)
    for copy in outs:
        copy.wait()


def main_call(recv, c, h, cf, sp, gs, w1, w2, bdeg, hdeg):
    return pl.pallas_call(
        main_kernel,
        in_specs=[vmem_spec()] + [hbm_spec()] * 5 + [vmem_spec()] * 4,
        out_specs=[hbm_spec(), vmem_spec(), vmem_spec()],
        out_shape=(
            pltpu.HBM((NB, HID), BF),
            pltpu.HBM((NH, HID), BF),
            jax.ShapeDtypeStruct((1024, 384), BF),
        ),
        scratch_shapes=[
            pltpu.VMEM((NH, NB), BF),
            pltpu.VMEM((NB, FEAT), F32),
            pltpu.VMEM((NB, NB), BF),
            pltpu.VMEM((NB, HID), F32),
            pltpu.VMEM((NB, HID), BF),
            pltpu.VMEM((NB, HID), BF),
            pltpu.VMEM((NB, HID), BF),
            pltpu.VMEM((NB, HID), F32),
            pltpu.VMEM((NB, FEAT), BF),
            pltpu.VMEM((NH, HID), BF),
            pltpu.VMEM((NH, HID), BF),
            pltpu.VMEM((FEAT, HID), F32),
            pltpu.VMEM((HID, HID), F32),
            pltpu.SemaphoreType.DMA((10,)),
        ],
        compiler_params=limit(58),
        name="main_part",
    )(keep(recv), leave(h), leave(cf), leave(c), leave(sp), leave(gs), w1, w2, bdeg, hdeg)


def tail_kernel(
    u_ref, w2_ref, bdeg_ref, ask_ref, pa_ref, out_hbm, hg_hbm, s_ref, out_ref, hg_ref, sems
):
    selector(ask_ref, s_ref)
    col = columns(lax.rsqrt(bdeg_ref[...].astype(F32)))
    copies = []
    for n, r in enumerate(range(0, NB, STEP)):
        at = slice(r, r + STEP)
        out_ref[at] = scale_rows(dot(u_ref[at], w2_ref[...]), col[at]).astype(BF)
        hg_ref[at] = dot_tl(s_ref[:, at], pa_ref[...]).astype(BF)
        for m, (src, dst) in enumerate(((out_ref, out_hbm), (hg_ref, hg_hbm))):
            copies.append(pltpu.make_async_copy(src.at[at], dst.at[at], sems.at[2 * n + m]))
            copies[-1].start()
    for copy in copies:
        copy.wait()


def tail_call(u, w2, bdeg, asked, pa):
    return pl.pallas_call(
        tail_kernel,
        in_specs=[vmem_spec()] * 5,
        out_specs=[hbm_spec()] * 2,
        out_shape=(
            jax.ShapeDtypeStruct((NB, HID), BF),
            jax.ShapeDtypeStruct((NB, HID), BF),
        ),
        scratch_shapes=[
            pltpu.VMEM((NH, NB), BF),
            pltpu.VMEM((NB, HID), BF),
            pltpu.VMEM((NB, HID), BF),
            pltpu.SemaphoreType.DMA((8,)),
        ],
        compiler_params=limit(58),
        name="tail_part",
    )(u, w2, bdeg, keep(asked), pa)


def sum_kernel(x_ref, o_ref):
    total = jnp.sum(x_ref[...].astype(F32), axis=0)
    o_ref[...] = jnp.broadcast_to(total.astype(BF)[None], (128, 8, 384))


def sum_call(x):
    return pl.pallas_call(
        sum_kernel,
        in_specs=[vmem_spec()],
        out_specs=vmem_spec(),
        out_shape=jax.ShapeDtypeStruct((128, 8, 384), BF),
        name="sum_part",
    )(keep(x))


def final_kernel(x_ref, g1_ref, g2_ref):
    factor = 1.0 / 512.0
    g2_ref[:, 0:256] = x_ref[0:512, 0:256].astype(F32) * factor
    g2_ref[:, 256:512] = x_ref[512:1024, 0:256].astype(F32) * factor
    for q in range(4):
        part = x_ref[128 * q : 128 * q + 128, 256:384].astype(F32)
        g1_ref[:, 128 * q : 128 * q + 128] = part * factor


def final_call(x):
    return pl.pallas_call(
        final_kernel,
        in_specs=[vmem_spec()],
        out_specs=[vmem_spec()] * 2,
        out_shape=(
            jax.ShapeDtypeStruct((FEAT, HID), F32),
            jax.ShapeDtypeStruct((HID, HID), F32),
        ),
        name="final_part",
    )(keep(x))


def exchange(x):
    return lax.all_to_all(x, AXES, split_axis=0, concat_axis=0, tiled=True)


def local(
    node_feats, batch_deg, batch_nbrs, halo_nbrs, halo_len, halo_rows, halo_deg,
    feat_table, emb_table, grad_table, weight_one, weight_two, grad_out,
):
    bdeg = batch_deg.reshape(1, NB)
    hdeg = halo_deg.reshape(1, NH)
    asked = exchange(halo_rows.reshape(128, 1, 4))
    h, gs, p = halo_call(halo_nbrs.T, halo_len.reshape(1, NB), bdeg, hdeg, grad_out)
    send = pick_call(asked, feat_table, emb_table, grad_table, p)
    recv = exchange(send.reshape(128, 8, 896)).reshape(1024, 896)
    c, cf, sp = batch_call(batch_nbrs.T, bdeg, node_feats, gs)
    u, pa, grads = main_call(recv, c, h, cf, sp, gs, weight_one, weight_two, bdeg, hdeg)
    shares = exchange(grads.reshape(128, 8, 384))
    out_embed, halo_grad = tail_call(u, weight_two, bdeg, asked, pa)
    sums = exchange(sum_call(shares)).reshape(1024, 384)
    grad_one, grad_two = final_call(sums)
    return out_embed, halo_grad, grad_one, grad_two


def solution(mesh):
    rows = P(AXES, None)
    flat = P(AXES)
    return jax.shard_map(
        local,
        mesh=mesh,
        in_specs=(
            rows, flat, rows, rows, flat, flat, flat, rows, rows, rows, P(), P(), rows,
        ),
        out_specs=(rows, rows, P(), P()),
        check_vma=False,
    )
```

```python
import jax
import jax.numpy as jnp
from jax import lax
from jax.experimental import pallas as pl
from jax.experimental.pallas import tpu as pltpu
from jax.sharding import PartitionSpec as P

BF = jnp.bfloat16
F32 = jnp.float32
AXES = ("dp", "mp")
NB = 2048
NH = 512
HID = 512
FEAT = 128
STEP = 512


def hbm_spec():
    return pl.BlockSpec(memory_space=pltpu.HBM)


def vmem_spec():
    return pl.BlockSpec(memory_space=pltpu.VMEM)


def held(*shape, dtype=BF):
    return pltpu.VMEM(shape, dtype)


def keep(x):
    return pltpu.with_memory_space_constraint(x, pltpu.VMEM)


def leave(x):
    return pltpu.with_memory_space_constraint(x, pltpu.HBM)


def limit(mib):
    return pltpu.CompilerParams(vmem_limit_bytes=mib * 1024 * 1024)


def dot(left, right):
    return jnp.dot(left, right, preferred_element_type=F32)


def dot_t(left, right):
    return lax.dot_general(left, right, (((1,), (1,)), ((), ())), preferred_element_type=F32)


def dot_tl(left, right):
    return lax.dot_general(left, right, (((0,), (0,)), ((), ())), preferred_element_type=F32)


def columns(row):
    n = row.shape[1]
    return jnp.concatenate(
        [jnp.broadcast_to(row[:, s : s + 128], (128, 128)).T for s in range(0, n, 128)], axis=0
    )


def scale_rows(x, col):
    reps = x.shape[1] // 128
    return x * (jnp.tile(col, (1, reps)) if reps > 1 else col)


def count_tiles(dst_ref, nbrs, rows0, n_rows):
    times = jnp.ones(nbrs.shape, jnp.int32)
    for k in range(1, 8):
        times = times + (nbrs == pltpu.roll(nbrs, k, 0)).astype(jnp.int32)
    times = times.astype(F32)
    zero = jnp.zeros((16, 128), BF)
    sub = lax.broadcasted_iota(jnp.int32, (16, 128), 0)
    for c in range(0, nbrs.shape[1], 128):
        idx = [
            jnp.broadcast_to(nbrs[k : k + 1, c : c + 128], (16, 128)).astype(jnp.int16)
            for k in range(8)
        ]
        val = [jnp.broadcast_to(times[k : k + 1, c : c + 128], (16, 128)).astype(BF) for k in range(8)]

        def group(t, _):
            base = pl.multiple_of(t * 128, 128)
            first = (sub + (base + rows0)).astype(jnp.int16)
            for r in range(0, 128, 16):
                here = first + jnp.int16(r)
                acc = zero
                for k in range(8):
                    acc = jnp.where(idx[k] == here, val[k], acc)
                dst_ref[pl.ds(base + r, 16), c : c + 128] = acc
            return 0

        lax.fori_loop(0, n_rows // 128, group, 0)


def halo_kernel(
    hn_ref, hl_ref, bdeg_ref, hdeg_ref, g_hbm, h_hbm, gs_hbm, p_ref, g_ref, h_ref, gs_ref, sems
):
    copy_in = pltpu.make_async_copy(g_hbm, g_ref, sems.at[0])
    copy_in.start()
    nbrs = hn_ref[...]
    slot = lax.broadcasted_iota(jnp.int32, nbrs.shape, 0)
    nbrs = jnp.where(slot < hl_ref[...], nbrs, -1)
    count_tiles(h_ref, nbrs, 0, NH)
    copy_h = pltpu.make_async_copy(h_ref, h_hbm, sems.at[1])
    copy_h.start()
    inv = columns(lax.rsqrt(bdeg_ref[...].astype(F32)))
    inv_h = columns(lax.rsqrt(hdeg_ref[...].astype(F32)))
    copy_in.wait()
    for s in range(0, NB, STEP):
        gs = scale_rows(g_ref[s : s + STEP, :].astype(F32), inv[s : s + STEP])
        gs_ref[s : s + STEP, :] = gs.astype(BF)
    copy_gs = pltpu.make_async_copy(gs_ref, gs_hbm, sems.at[2])
    copy_gs.start()
    p_ref[...] = scale_rows(dot(h_ref[...], gs_ref[...]), inv_h).astype(BF)
    copy_h.wait()
    copy_gs.wait()


def halo_call(hn, hl, bdeg, hdeg, g):
    return pl.pallas_call(
        halo_kernel,
        in_specs=[vmem_spec()] * 4 + [hbm_spec()],
        out_specs=[hbm_spec(), hbm_spec(), vmem_spec()],
        out_shape=(
            pltpu.HBM((NH, NB), BF),
            pltpu.HBM((NB, HID), BF),
            held(NH, HID),
        ),
        scratch_shapes=[
            pltpu.VMEM((NB, HID), BF),
            pltpu.VMEM((NH, NB), BF),
            pltpu.VMEM((NB, HID), BF),
            pltpu.SemaphoreType.DMA((3,)),
        ],
        compiler_params=limit(58),
        name="halo_part",
    )(hn, hl, bdeg, hdeg, leave(g))


def pair_up(top, bottom):
    w = top.shape[1]
    t = top.reshape(64, 8, w)
    b = bottom.reshape(64, 8, w)
    low = lax.broadcasted_iota(jnp.int32, (64, 8, w), 1) < 4
    even = jnp.where(low, t, pltpu.roll(b, 4, 1))
    odd = jnp.where(low, pltpu.roll(t, 4, 1), b)
    return jnp.concatenate([even, odd], axis=1).astype(BF).reshape(1024, w)


def part_up(both):
    w = both.shape[1]
    x = both.reshape(64, 16, w).astype(F32)
    even, odd = x[:, 0:8], x[:, 8:16]
    low = lax.broadcasted_iota(jnp.int32, (64, 8, w), 1) < 4
    top = jnp.where(low, even, pltpu.roll(odd, 4, 1))
    bottom = jnp.where(low, pltpu.roll(even, 4, 1), odd)
    return top.reshape(512, w), bottom.reshape(512, w)


def selector(ask_ref, s_ref):
    a = ask_ref[...].reshape(64, 2, 1, 4)
    sub = lax.broadcasted_iota(jnp.int32, (64, 8, 4), 1)
    lane = lax.broadcasted_iota(jnp.int32, (64, 8, 4), 2)
    mine = jnp.where(
        sub < 4, jnp.broadcast_to(a[:, 0], (64, 8, 4)), jnp.broadcast_to(a[:, 1], (64, 8, 4))
    )
    mine = jnp.where(lane == (sub & 3), mine & (NB - 1), 0)
    col = jnp.sum(mine.astype(F32), axis=2, keepdims=True).reshape(512, 1).astype(jnp.int32)
    colb = jnp.broadcast_to(col, (512, 128))
    lanes = lax.broadcasted_iota(jnp.int32, (512, 128), 1)
    for c in range(0, NB, 128):
        s_ref[:, c : c + 128] = jnp.where(colb == lanes + c, 1.0, 0.0).astype(BF)


def pick_kernel(
    ask_ref, x_hbm, e_hbm, v_hbm, p_ref, out_hbm, s_ref, x_ref, e_ref, v_ref, out_ref, sems
):
    copies = [
        pltpu.make_async_copy(src, dst, sems.at[n])
        for n, (src, dst) in enumerate(((e_hbm, e_ref), (v_hbm, v_ref), (x_hbm, x_ref)))
    ]
    for copy in copies:
        copy.start()
    selector(ask_ref, s_ref)
    s = s_ref[...]
    copies[0].wait()
    picked = dot(s, e_ref[...])
    copies[1].wait()
    out_ref[:, 0:512] = pair_up(picked, dot(s, v_ref[...]))
    left = pltpu.make_async_copy(out_ref.at[:, 0:512], out_hbm.at[:, 0:512], sems.at[3])
    left.start()
    copies[2].wait()
    p = p_ref[...].astype(F32)
    out_ref[:, 512:640] = pair_up(dot(s, x_ref[...]), p[:, 0:128])
    out_ref[:, 640:768] = pair_up(p[:, 128:256], p[:, 256:384])
    out_ref[:, 768:896] = pair_up(p[:, 384:512], p[:, 384:512])
    right = pltpu.make_async_copy(out_ref.at[:, 512:896], out_hbm.at[:, 512:896], sems.at[4])
    right.start()
    left.wait()
    right.wait()


def pick_call(asked, x, e, v, p):
    return pl.pallas_call(
        pick_kernel,
        in_specs=[vmem_spec(), hbm_spec(), hbm_spec(), hbm_spec(), vmem_spec()],
        out_specs=hbm_spec(),
        out_shape=pltpu.HBM((1024, 896), BF),
        scratch_shapes=[
            pltpu.VMEM((NH, NB), BF),
            pltpu.VMEM((NB, FEAT), BF),
            pltpu.VMEM((NB, HID), BF),
            pltpu.VMEM((NB, HID), BF),
            pltpu.VMEM((1024, 896), BF),
            pltpu.SemaphoreType.DMA((5,)),
        ],
        compiler_params=limit(58),
        name="pick_rows",
    )(keep(asked), leave(x), leave(e), leave(v), keep(p))


def batch_kernel(
    nb_ref, bdeg_ref, f_ref, gs_ref, w2_ref, c_hbm, cf_ref, sp_hbm, bp_hbm,
    fs_ref, c_ref, sp_ref, bp_ref, sems,
):
    col = columns(lax.rsqrt(bdeg_ref[...].astype(F32)))
    fs_ref[...] = (f_ref[...].astype(F32) * col).astype(BF)
    eye = (
        lax.broadcasted_iota(jnp.int32, (128, 128), 0)
        == lax.broadcasted_iota(jnp.int32, (128, 128), 1)
    ).astype(F32).astype(BF)
    count_tiles(c_ref, nb_ref[...], 0, NB)
    for r in range(0, NB, 128):
        c_ref[r : r + 128, r : r + 128] = c_ref[r : r + 128, r : r + 128] + eye
    copies = [pltpu.make_async_copy(c_ref, c_hbm, sems.at[0])]
    copies[0].start()
    for n, r in enumerate(range(0, NB, STEP)):
        at = slice(r, r + STEP)
        spread = dot(c_ref[at, :], gs_ref[...]).astype(BF)
        sp_ref[at, :] = spread
        bp_ref[at, :] = dot_t(spread, w2_ref[...])
        for m, (src, dst) in enumerate(((sp_ref, sp_hbm), (bp_ref, bp_hbm))):
            copies.append(pltpu.make_async_copy(src.at[at], dst.at[at], sems.at[1 + 2 * n + m]))
            copies[-1].start()
        cf_ref[at, :] = dot_tl(c_ref[:, at], fs_ref[...])
    for copy in copies:
        copy.wait()


def batch_call(nb, bdeg, f, gs, w2):
    return pl.pallas_call(
        batch_kernel,
        in_specs=[vmem_spec()] * 5,
        out_specs=[hbm_spec(), vmem_spec(), hbm_spec(), hbm_spec()],
        out_shape=(
            pltpu.HBM((NB, NB), BF),
            pltpu.HBM((NB, FEAT), F32),
            pltpu.HBM((NB, HID), BF),
            pltpu.HBM((NB, HID), F32),
        ),
        scratch_shapes=[
            pltpu.VMEM((NB, FEAT), BF),
            pltpu.VMEM((NB, NB), BF),
            pltpu.VMEM((NB, HID), BF),
            pltpu.VMEM((NB, HID), F32),
            pltpu.SemaphoreType.DMA((9,)),
        ],
        compiler_params=limit(58),
        name="batch_part",
    )(nb, bdeg, f, gs, w2)


def main_kernel(
    r_ref, h_hbm, cf_hbm, sp_hbm, bp_hbm, p_ref, w1_ref, w2_ref, bdeg_ref, hdeg_ref,
    hid_hbm, grads_ref,
    h_ref, cf_ref, sp_ref, bp_ref, hid_ref, g1_ref, g2_ref, sems,
):
    pairs = ((h_hbm, h_ref), (cf_hbm, cf_ref), (bp_hbm, bp_ref), (sp_hbm, sp_ref))
    copies = [pltpu.make_async_copy(src, dst, sems.at[n]) for n, (src, dst) in enumerate(pairs)]
    for copy in copies[:2]:
        copy.start()
    inv = columns(lax.rsqrt(bdeg_ref[...].astype(F32)))
    col_h = columns(lax.rsqrt(hdeg_ref[...].astype(F32)))
    hx, _ = part_up(r_ref[:, 512:640])
    hx = (hx * col_h).astype(BF)
    he, hv = part_up(r_ref[:, 0:512])
    hvw = scale_rows(dot_t(hv.astype(BF), w2_ref[...]), col_h).astype(BF)
    g2_ref[...] = dot_tl(he.astype(BF), p_ref[...])
    for copy in copies[:2]:
        copy.wait()
    for copy in copies[2:]:
        copy.start()
    outs = []
    for n, s in enumerate(range(0, NB, STEP)):
        at = slice(s, s + STEP)
        col = inv[at]
        h = h_ref[:, at]
        u1 = (cf_ref[at, :] + dot_tl(h, hx)).astype(BF)
        pre = scale_rows(dot(u1, w1_ref[...]), col)
        sig = 0.5 + 0.5 * jnp.tanh(0.5 * pre)
        hid_ref[at, :] = scale_rows(pre * sig, col).astype(BF)
        outs.append(pltpu.make_async_copy(hid_ref.at[at], hid_hbm.at[at], sems.at[4 + n]))
        outs[-1].start()
        der = scale_rows(sig * (1.0 + pre * (1.0 - sig)), col * col)
        if n == 0:
            copies[2].wait()
        d_pre = ((bp_ref[at, :] + dot_tl(h, hvw)) * der).astype(BF)
        g1 = dot_tl(u1, d_pre)
        if n == 0:
            copies[3].wait()
            g1_ref[...] = g1
        else:
            g1_ref[...] += g1
    g2_ref[...] += dot_tl(hid_ref[...], sp_ref[...])
    grads_ref[0:512, 0:256] = g2_ref[:, 0:256].astype(BF)
    grads_ref[512:1024, 0:256] = g2_ref[:, 256:512].astype(BF)
    for q in range(4):
        grads_ref[128 * q : 128 * q + 128, 256:384] = g1_ref[:, 128 * q : 128 * q + 128].astype(BF)
    grads_ref[512:1024, 256:384] = jnp.zeros((512, 128), BF)
    for copy in outs:
        copy.wait()


def main_call(recv, h, cf, sp, bp, p, w1, w2, bdeg, hdeg):
    return pl.pallas_call(
        main_kernel,
        in_specs=[vmem_spec()] + [hbm_spec()] * 4 + [vmem_spec()] * 5,
        out_specs=[hbm_spec(), vmem_spec()],
        out_shape=(pltpu.HBM((NB, HID), BF), jax.ShapeDtypeStruct((1024, 384), BF)),
        scratch_shapes=[
            pltpu.VMEM((NH, NB), BF),
            pltpu.VMEM((NB, FEAT), F32),
            pltpu.VMEM((NB, HID), BF),
            pltpu.VMEM((NB, HID), F32),
            pltpu.VMEM((NB, HID), BF),
            pltpu.VMEM((FEAT, HID), F32),
            pltpu.VMEM((HID, HID), F32),
            pltpu.SemaphoreType.DMA((8,)),
        ],
        compiler_params=limit(58),
        name="main_part",
    )(keep(recv), leave(h), leave(cf), leave(sp), leave(bp), keep(p), w1, w2, bdeg, hdeg)


def out_kernel(
    r_ref, c_hbm, h_hbm, hid_ref, w2_ref, bdeg_ref, hdeg_ref, out_hbm,
    c_ref, h_ref, he_ref, out_ref, sems,
):
    ins = [
        pltpu.make_async_copy(c_hbm, c_ref, sems.at[0]),
        pltpu.make_async_copy(h_hbm, h_ref, sems.at[1]),
    ]
    for copy in ins:
        copy.start()
    inv = columns(lax.rsqrt(bdeg_ref[...].astype(F32)))
    col_h = columns(lax.rsqrt(hdeg_ref[...].astype(F32)))
    he, _ = part_up(r_ref[:, 0:512])
    he_ref[...] = scale_rows(he, col_h).astype(BF)
    for copy in ins:
        copy.wait()
    outs = []
    for n, s in enumerate(range(0, NB, STEP)):
        at = slice(s, s + STEP)
        u = dot_tl(c_ref[:, at], hid_ref[...]) + dot_tl(h_ref[:, at], he_ref[...])
        out_ref[at] = scale_rows(dot(u.astype(BF), w2_ref[...]), inv[at]).astype(BF)
        outs.append(pltpu.make_async_copy(out_ref.at[at], out_hbm.at[at], sems.at[2 + n]))
        outs[-1].start()
    for copy in outs:
        copy.wait()


def out_call(recv, c, h, hid, w2, bdeg, hdeg):
    return pl.pallas_call(
        out_kernel,
        in_specs=[vmem_spec(), hbm_spec(), hbm_spec()] + [vmem_spec()] * 4,
        out_specs=hbm_spec(),
        out_shape=jax.ShapeDtypeStruct((NB, HID), BF),
        scratch_shapes=[
            pltpu.VMEM((NB, NB), BF),
            pltpu.VMEM((NH, NB), BF),
            pltpu.VMEM((NH, HID), BF),
            pltpu.VMEM((NB, HID), BF),
            pltpu.SemaphoreType.DMA((6,)),
        ],
        compiler_params=limit(58),
        name="out_part",
    )(keep(recv), leave(c), leave(h), hid, w2, bdeg, hdeg)


def tail_kernel(ask_ref, r_ref, hg_hbm, s_ref, pa_ref, hg_ref, sems):
    selector(ask_ref, s_ref)
    _, p0 = part_up(r_ref[:, 512:640])
    p1, p2 = part_up(r_ref[:, 640:768])
    p3, _ = part_up(r_ref[:, 768:896])
    for q, part in enumerate((p0, p1, p2, p3)):
        pa_ref[:, 128 * q : 128 * q + 128] = part.astype(BF)
    copies = []
    for n, r in enumerate(range(0, NB, STEP)):
        at = slice(r, r + STEP)
        hg_ref[at] = dot_tl(s_ref[:, at], pa_ref[...]).astype(BF)
        copies.append(pltpu.make_async_copy(hg_ref.at[at], hg_hbm.at[at], sems.at[n]))
        copies[-1].start()
    for copy in copies:
        copy.wait()


def tail_call(asked, recv):
    return pl.pallas_call(
        tail_kernel,
        in_specs=[vmem_spec()] * 2,
        out_specs=hbm_spec(),
        out_shape=jax.ShapeDtypeStruct((NB, HID), BF),
        scratch_shapes=[
            pltpu.VMEM((NH, NB), BF),
            pltpu.VMEM((NH, HID), BF),
            pltpu.VMEM((NB, HID), BF),
            pltpu.SemaphoreType.DMA((4,)),
        ],
        compiler_params=limit(58),
        name="tail_part",
    )(keep(asked), keep(recv))


def sum_kernel(x_ref, o_ref):
    total = jnp.sum(x_ref[...].astype(F32), axis=0)
    o_ref[...] = jnp.broadcast_to(total.astype(BF)[None], (128, 8, 384))


def sum_call(x):
    return pl.pallas_call(
        sum_kernel,
        in_specs=[vmem_spec()],
        out_specs=vmem_spec(),
        out_shape=jax.ShapeDtypeStruct((128, 8, 384), BF),
        name="sum_part",
    )(keep(x))


def final_kernel(x_ref, g1_ref, g2_ref):
    factor = 1.0 / 512.0
    g2_ref[:, 0:256] = x_ref[0:512, 0:256].astype(F32) * factor
    g2_ref[:, 256:512] = x_ref[512:1024, 0:256].astype(F32) * factor
    for q in range(4):
        part = x_ref[128 * q : 128 * q + 128, 256:384].astype(F32)
        g1_ref[:, 128 * q : 128 * q + 128] = part * factor


def final_call(x):
    return pl.pallas_call(
        final_kernel,
        in_specs=[vmem_spec()],
        out_specs=[vmem_spec()] * 2,
        out_shape=(
            jax.ShapeDtypeStruct((FEAT, HID), F32),
            jax.ShapeDtypeStruct((HID, HID), F32),
        ),
        name="final_part",
    )(keep(x))


def exchange(x):
    return lax.all_to_all(x, AXES, split_axis=0, concat_axis=0, tiled=True)


def local(
    node_feats, batch_deg, batch_nbrs, halo_nbrs, halo_len, halo_rows, halo_deg,
    feat_table, emb_table, grad_table, weight_one, weight_two, grad_out,
):
    bdeg = batch_deg.reshape(1, NB)
    hdeg = halo_deg.reshape(1, NH)
    asked = exchange(halo_rows.reshape(128, 1, 4))
    h, gs, p = halo_call(halo_nbrs.T, halo_len.reshape(1, NB), bdeg, hdeg, grad_out)
    send = pick_call(asked, feat_table, emb_table, grad_table, p)
    recv = exchange(send.reshape(128, 8, 896)).reshape(1024, 896)
    c, cf, sp, bp = batch_call(batch_nbrs.T, bdeg, node_feats, gs, weight_two)
    hid, grads = main_call(recv, h, cf, sp, bp, p, weight_one, weight_two, bdeg, hdeg)
    shares = exchange(grads.reshape(128, 8, 384))
    out_embed = out_call(recv, c, h, hid, weight_two, bdeg, hdeg)
    shares, out_embed = lax.optimization_barrier((shares, out_embed))
    sums = exchange(sum_call(shares)).reshape(1024, 384)
    halo_grad = tail_call(asked, recv)
    grad_one, grad_two = final_call(sums)
    return out_embed, halo_grad, grad_one, grad_two


def solution(mesh):
    rows = P(AXES, None)
    flat = P(AXES)
    return jax.shard_map(
        local,
        mesh=mesh,
        in_specs=(
            rows, flat, rows, rows, flat, flat, flat, rows, rows, rows, P(), P(), rows,
        ),
        out_specs=(rows, rows, P(), P()),
        check_vma=False,
    )
```

```python
import jax
import jax.numpy as jnp
from jax import lax
from jax.experimental import pallas as pl
from jax.experimental.pallas import tpu as pltpu
from jax.sharding import PartitionSpec as P

BF = jnp.bfloat16
F32 = jnp.float32
AXES = ("dp", "mp")
NB = 2048
NH = 512
HID = 512
FEAT = 128
STEP = 512


def hbm_spec():
    return pl.BlockSpec(memory_space=pltpu.HBM)


def vmem_spec():
    return pl.BlockSpec(memory_space=pltpu.VMEM)


def held(*shape, dtype=BF):
    return pltpu.VMEM(shape, dtype)


def keep(x):
    return pltpu.with_memory_space_constraint(x, pltpu.VMEM)


def leave(x):
    return pltpu.with_memory_space_constraint(x, pltpu.HBM)


def limit(mib):
    return pltpu.CompilerParams(vmem_limit_bytes=mib * 1024 * 1024)


def dot(left, right):
    return jnp.dot(left, right, preferred_element_type=F32)


def dot_t(left, right):
    return lax.dot_general(left, right, (((1,), (1,)), ((), ())), preferred_element_type=F32)


def dot_tl(left, right):
    return lax.dot_general(left, right, (((0,), (0,)), ((), ())), preferred_element_type=F32)


def columns(row):
    n = row.shape[1]
    return jnp.concatenate(
        [jnp.broadcast_to(row[:, s : s + 128], (128, 128)).T for s in range(0, n, 128)], axis=0
    )


def scale_rows(x, col):
    reps = x.shape[1] // 128
    return x * (jnp.tile(col, (1, reps)) if reps > 1 else col)


def count_tiles(dst_ref, nbrs, rows0, n_rows):
    times = jnp.ones(nbrs.shape, jnp.int32)
    for k in range(1, 8):
        times = times + (nbrs == pltpu.roll(nbrs, k, 0)).astype(jnp.int32)
    times = times.astype(F32)
    zero = jnp.zeros((16, 128), BF)
    sub = lax.broadcasted_iota(jnp.int32, (16, 128), 0)
    for c in range(0, nbrs.shape[1], 128):
        idx = [
            jnp.broadcast_to(nbrs[k : k + 1, c : c + 128], (16, 128)).astype(jnp.int16)
            for k in range(8)
        ]
        val = [jnp.broadcast_to(times[k : k + 1, c : c + 128], (16, 128)).astype(BF) for k in range(8)]

        def group(t, _):
            base = pl.multiple_of(t * 128, 128)
            first = (sub + (base + rows0)).astype(jnp.int16)
            for r in range(0, 128, 16):
                here = first + jnp.int16(r)
                acc = zero
                for k in range(8):
                    acc = jnp.where(idx[k] == here, val[k], acc)
                dst_ref[pl.ds(base + r, 16), c : c + 128] = acc
            return 0

        lax.fori_loop(0, n_rows // 128, group, 0)


def halo_kernel(
    hn_ref, hl_ref, bdeg_ref, hdeg_ref, g_hbm, h_hbm, gs_hbm, p_ref, g_ref, h_ref, gs_ref, sems
):
    copy_in = pltpu.make_async_copy(g_hbm, g_ref, sems.at[0])
    copy_in.start()
    nbrs = hn_ref[...]
    slot = lax.broadcasted_iota(jnp.int32, nbrs.shape, 0)
    nbrs = jnp.where(slot < hl_ref[...], nbrs, -1)
    count_tiles(h_ref, nbrs, 0, NH)
    copy_h = pltpu.make_async_copy(h_ref, h_hbm, sems.at[1])
    copy_h.start()
    inv = columns(lax.rsqrt(bdeg_ref[...].astype(F32)))
    inv_h = columns(lax.rsqrt(hdeg_ref[...].astype(F32)))
    copy_in.wait()
    for s in range(0, NB, STEP):
        gs = scale_rows(g_ref[s : s + STEP, :].astype(F32), inv[s : s + STEP])
        gs_ref[s : s + STEP, :] = gs.astype(BF)
    copy_gs = pltpu.make_async_copy(gs_ref, gs_hbm, sems.at[2])
    copy_gs.start()
    p_ref[...] = scale_rows(dot(h_ref[...], gs_ref[...]), inv_h).astype(BF)
    copy_h.wait()
    copy_gs.wait()


def halo_call(hn, hl, bdeg, hdeg, g):
    return pl.pallas_call(
        halo_kernel,
        in_specs=[vmem_spec()] * 4 + [hbm_spec()],
        out_specs=[hbm_spec(), hbm_spec(), vmem_spec()],
        out_shape=(
            pltpu.HBM((NH, NB), BF),
            pltpu.HBM((NB, HID), BF),
            held(NH, HID),
        ),
        scratch_shapes=[
            pltpu.VMEM((NB, HID), BF),
            pltpu.VMEM((NH, NB), BF),
            pltpu.VMEM((NB, HID), BF),
            pltpu.SemaphoreType.DMA((3,)),
        ],
        compiler_params=limit(58),
        name="halo_part",
    )(hn, hl, bdeg, hdeg, leave(g))


def rows_of(ref, lo, hi):
    return ref[:, :, lo:hi].reshape(NH, hi - lo)


def chunks_of(x):
    return x.astype(BF).reshape(x.shape[0] // 4, 4, x.shape[1])


def selector(ask_ref, s_ref):
    a = ask_ref[...].reshape(64, 2, 1, 4)
    sub = lax.broadcasted_iota(jnp.int32, (64, 8, 4), 1)
    lane = lax.broadcasted_iota(jnp.int32, (64, 8, 4), 2)
    mine = jnp.where(
        sub < 4, jnp.broadcast_to(a[:, 0], (64, 8, 4)), jnp.broadcast_to(a[:, 1], (64, 8, 4))
    )
    mine = jnp.where(lane == (sub & 3), mine & (NB - 1), 0)
    col = jnp.sum(mine.astype(F32), axis=2, keepdims=True).reshape(512, 1).astype(jnp.int32)
    colb = jnp.broadcast_to(col, (512, 128))
    lanes = lax.broadcasted_iota(jnp.int32, (512, 128), 1)
    for c in range(0, NB, 128):
        s_ref[:, c : c + 128] = jnp.where(colb == lanes + c, 1.0, 0.0).astype(BF)


def pick_kernel(
    ask_ref, x_hbm, e_hbm, v_hbm, p_ref, out_hbm, s_ref, x_ref, e_ref, v_ref, out_ref, sems
):
    copies = [
        pltpu.make_async_copy(src, dst, sems.at[n])
        for n, (src, dst) in enumerate(((e_hbm, e_ref), (v_hbm, v_ref), (x_hbm, x_ref)))
    ]
    for copy in copies:
        copy.start()
    out_ref[:, :, 1152:1664] = chunks_of(p_ref[...])
    selector(ask_ref, s_ref)
    s = s_ref[...]
    sends = []
    for n, (lo, hi, src) in enumerate(((128, 640, e_ref), (640, 1152, v_ref), (0, 128, x_ref))):
        copies[n].wait()
        out_ref[:, :, lo:hi] = chunks_of(dot(s, src[...]))
        if n == 1:
            hi = 1664
        at = (slice(None), slice(None), slice(lo, hi))
        sends.append(pltpu.make_async_copy(out_ref.at[at], out_hbm.at[at], sems.at[3 + n]))
        sends[-1].start()
    for copy in sends:
        copy.wait()


def pick_call(asked, x, e, v, p):
    return pl.pallas_call(
        pick_kernel,
        in_specs=[vmem_spec(), hbm_spec(), hbm_spec(), hbm_spec(), vmem_spec()],
        out_specs=hbm_spec(),
        out_shape=pltpu.HBM((128, 4, 1664), BF),
        scratch_shapes=[
            pltpu.VMEM((NH, NB), BF),
            pltpu.VMEM((NB, FEAT), BF),
            pltpu.VMEM((NB, HID), BF),
            pltpu.VMEM((NB, HID), BF),
            pltpu.VMEM((128, 4, 1664), BF),
            pltpu.SemaphoreType.DMA((6,)),
        ],
        compiler_params=limit(58),
        name="pick_rows",
    )(keep(asked), leave(x), leave(e), leave(v), keep(p))


def batch_kernel(
    nb_ref, bdeg_ref, f_ref, gs_ref, w2_ref, c_hbm, cf_ref, sp_hbm, bp_hbm,
    fs_ref, c_ref, sp_ref, bp_ref, sems,
):
    col = columns(lax.rsqrt(bdeg_ref[...].astype(F32)))
    fs_ref[...] = (f_ref[...].astype(F32) * col).astype(BF)
    eye = (
        lax.broadcasted_iota(jnp.int32, (128, 128), 0)
        == lax.broadcasted_iota(jnp.int32, (128, 128), 1)
    ).astype(F32).astype(BF)
    count_tiles(c_ref, nb_ref[...], 0, NB)
    for r in range(0, NB, 128):
        c_ref[r : r + 128, r : r + 128] = c_ref[r : r + 128, r : r + 128] + eye
    copies = [pltpu.make_async_copy(c_ref, c_hbm, sems.at[0])]
    copies[0].start()
    for n, r in enumerate(range(0, NB, STEP)):
        at = slice(r, r + STEP)
        spread = dot(c_ref[at, :], gs_ref[...]).astype(BF)
        sp_ref[at, :] = spread
        bp_ref[at, :] = dot_t(spread, w2_ref[...])
        for m, (src, dst) in enumerate(((sp_ref, sp_hbm), (bp_ref, bp_hbm))):
            copies.append(pltpu.make_async_copy(src.at[at], dst.at[at], sems.at[1 + 2 * n + m]))
            copies[-1].start()
        cf_ref[at, :] = dot_tl(c_ref[:, at], fs_ref[...])
    for copy in copies:
        copy.wait()


def batch_call(nb, bdeg, f, gs, w2):
    return pl.pallas_call(
        batch_kernel,
        in_specs=[vmem_spec()] * 5,
        out_specs=[hbm_spec(), vmem_spec(), hbm_spec(), hbm_spec()],
        out_shape=(
            pltpu.HBM((NB, NB), BF),
            pltpu.HBM((NB, FEAT), F32),
            pltpu.HBM((NB, HID), BF),
            pltpu.HBM((NB, HID), F32),
        ),
        scratch_shapes=[
            pltpu.VMEM((NB, FEAT), BF),
            pltpu.VMEM((NB, NB), BF),
            pltpu.VMEM((NB, HID), BF),
            pltpu.VMEM((NB, HID), F32),
            pltpu.SemaphoreType.DMA((9,)),
        ],
        compiler_params=limit(58),
        name="batch_part",
    )(nb, bdeg, f, gs, w2)


def main_kernel(
    r_ref, h_hbm, cf_hbm, sp_hbm, bp_hbm, p_ref, w1_ref, w2_ref, bdeg_ref, hdeg_ref,
    hid_hbm, grads_ref,
    h_ref, cf_ref, sp_ref, bp_ref, hid_ref, g1_ref, g2_ref, sems,
):
    pairs = ((h_hbm, h_ref), (cf_hbm, cf_ref), (bp_hbm, bp_ref), (sp_hbm, sp_ref))
    copies = [pltpu.make_async_copy(src, dst, sems.at[n]) for n, (src, dst) in enumerate(pairs)]
    for copy in copies[:2]:
        copy.start()
    inv = columns(lax.rsqrt(bdeg_ref[...].astype(F32)))
    col_h = columns(lax.rsqrt(hdeg_ref[...].astype(F32)))
    hx = (rows_of(r_ref, 0, 128).astype(F32) * col_h).astype(BF)
    hvw = scale_rows(dot_t(rows_of(r_ref, 640, 1152), w2_ref[...]), col_h).astype(BF)
    g2_ref[...] = dot_tl(rows_of(r_ref, 128, 640), p_ref[...])
    for copy in copies[:2]:
        copy.wait()
    for copy in copies[2:]:
        copy.start()
    outs = []
    for n, s in enumerate(range(0, NB, STEP)):
        at = slice(s, s + STEP)
        col = inv[at]
        h = h_ref[:, at]
        u1 = (cf_ref[at, :] + dot_tl(h, hx)).astype(BF)
        pre = scale_rows(dot(u1, w1_ref[...]), col)
        sig = 0.5 + 0.5 * jnp.tanh(0.5 * pre)
        hid_ref[at, :] = scale_rows(pre * sig, col).astype(BF)
        outs.append(pltpu.make_async_copy(hid_ref.at[at], hid_hbm.at[at], sems.at[4 + n]))
        outs[-1].start()
        der = scale_rows(sig * (1.0 + pre * (1.0 - sig)), col * col)
        if n == 0:
            copies[2].wait()
        d_pre = ((bp_ref[at, :] + dot_tl(h, hvw)) * der).astype(BF)
        g1 = dot_tl(u1, d_pre)
        if n == 0:
            copies[3].wait()
            g1_ref[...] = g1
        else:
            g1_ref[...] += g1
    g2_ref[...] += dot_tl(hid_ref[...], sp_ref[...])
    grads_ref[:, :, 0:512] = chunks_of(g2_ref[...])
    for q in range(4):
        part = g1_ref[:, 128 * q : 128 * q + 128]
        grads_ref[32 * q : 32 * q + 32, :, 512:640] = chunks_of(part)
    for copy in outs:
        copy.wait()


def main_call(recv, h, cf, sp, bp, p, w1, w2, bdeg, hdeg):
    return pl.pallas_call(
        main_kernel,
        in_specs=[vmem_spec()] + [hbm_spec()] * 4 + [vmem_spec()] * 5,
        out_specs=[hbm_spec(), vmem_spec()],
        out_shape=(pltpu.HBM((NB, HID), BF), jax.ShapeDtypeStruct((128, 4, 640), BF)),
        scratch_shapes=[
            pltpu.VMEM((NH, NB), BF),
            pltpu.VMEM((NB, FEAT), F32),
            pltpu.VMEM((NB, HID), BF),
            pltpu.VMEM((NB, HID), F32),
            pltpu.VMEM((NB, HID), BF),
            pltpu.VMEM((FEAT, HID), F32),
            pltpu.VMEM((HID, HID), F32),
            pltpu.SemaphoreType.DMA((8,)),
        ],
        compiler_params=limit(58),
        name="main_part",
    )(keep(recv), leave(h), leave(cf), leave(sp), leave(bp), keep(p), w1, w2, bdeg, hdeg)


def out_kernel(half, refs):
    r_ref, c_hbm, h_hbm, hid_ref, w2_ref, bdeg_ref, hdeg_ref = refs[:7]
    out_hbm, c_ref, h_ref, he_ref, out_ref, sems = refs[-6:]
    at = slice(half * NB // 2, (half + 1) * NB // 2)
    ins = [
        pltpu.make_async_copy(c_hbm.at[:, at], c_ref, sems.at[0]),
        pltpu.make_async_copy(h_hbm.at[:, at], h_ref, sems.at[1]),
    ]
    for copy in ins:
        copy.start()
    inv = columns(lax.rsqrt(bdeg_ref[:, at].astype(F32)))
    col_h = columns(lax.rsqrt(hdeg_ref[...].astype(F32)))
    he_ref[...] = scale_rows(rows_of(r_ref, 128, 640).astype(F32), col_h).astype(BF)
    for copy in ins:
        copy.wait()
    outs = []
    for n, s in enumerate(range(0, NB // 2, STEP)):
        here = slice(s, s + STEP)
        there = slice(at.start + s, at.start + s + STEP)
        u = dot_tl(c_ref[:, here], hid_ref[...]) + dot_tl(h_ref[:, here], he_ref[...])
        out_ref[here] = scale_rows(dot(u.astype(BF), w2_ref[...]), inv[here]).astype(BF)
        outs.append(pltpu.make_async_copy(out_ref.at[here], out_hbm.at[there], sems.at[2 + n]))
        outs[-1].start()
    for copy in outs:
        copy.wait()


def out_call(half, recv, c, h, hid, w2, bdeg, hdeg, *first):
    return pl.pallas_call(
        lambda *refs: out_kernel(half, refs),
        in_specs=[vmem_spec(), hbm_spec(), hbm_spec()] + [vmem_spec()] * 4 + [hbm_spec()] * len(first),
        out_specs=hbm_spec(),
        out_shape=pltpu.HBM((NB, HID), BF),
        input_output_aliases={7: 0} if first else {},
        scratch_shapes=[
            pltpu.VMEM((NB, NB // 2), BF),
            pltpu.VMEM((NH, NB // 2), BF),
            pltpu.VMEM((NH, HID), BF),
            pltpu.VMEM((NB // 2, HID), BF),
            pltpu.SemaphoreType.DMA((4,)),
        ],
        compiler_params=limit(58),
        name=f"out_part_{half}",
    )(keep(recv), leave(c), leave(h), hid, w2, bdeg, hdeg, *first)


def tail_kernel(ask_ref, r_ref, hg_hbm, s_ref, pa_ref, hg_ref, sems):
    selector(ask_ref, s_ref)
    pa_ref[...] = rows_of(r_ref, 1152, 1664)
    copies = []
    for n, r in enumerate(range(0, NB, STEP)):
        at = slice(r, r + STEP)
        hg_ref[at] = dot_tl(s_ref[:, at], pa_ref[...]).astype(BF)
        copies.append(pltpu.make_async_copy(hg_ref.at[at], hg_hbm.at[at], sems.at[n]))
        copies[-1].start()
    for copy in copies:
        copy.wait()


def tail_call(asked, recv):
    return pl.pallas_call(
        tail_kernel,
        in_specs=[vmem_spec()] * 2,
        out_specs=hbm_spec(),
        out_shape=jax.ShapeDtypeStruct((NB, HID), BF),
        scratch_shapes=[
            pltpu.VMEM((NH, NB), BF),
            pltpu.VMEM((NH, HID), BF),
            pltpu.VMEM((NB, HID), BF),
            pltpu.SemaphoreType.DMA((4,)),
        ],
        compiler_params=limit(58),
        name="tail_part",
    )(keep(asked), keep(recv))


def sum_kernel(x_ref, o_ref):
    total = jnp.sum(x_ref[...].astype(F32), axis=0)
    o_ref[...] = jnp.broadcast_to(total.astype(BF)[None], (128, 4, 640))


def sum_call(x):
    return pl.pallas_call(
        sum_kernel,
        in_specs=[vmem_spec()],
        out_specs=vmem_spec(),
        out_shape=jax.ShapeDtypeStruct((128, 4, 640), BF),
        name="sum_part",
    )(keep(x))


def final_kernel(x_ref, g1_ref, g2_ref):
    factor = 1.0 / 512.0
    g2_ref[...] = rows_of(x_ref, 0, 512).astype(F32) * factor
    for q in range(4):
        part = x_ref[32 * q : 32 * q + 32, :, 512:640].reshape(128, 128)
        g1_ref[:, 128 * q : 128 * q + 128] = part.astype(F32) * factor


def final_call(x):
    return pl.pallas_call(
        final_kernel,
        in_specs=[vmem_spec()],
        out_specs=[vmem_spec()] * 2,
        out_shape=(
            jax.ShapeDtypeStruct((FEAT, HID), F32),
            jax.ShapeDtypeStruct((HID, HID), F32),
        ),
        name="final_part",
    )(keep(x))


def exchange(x):
    return lax.all_to_all(x, AXES, split_axis=0, concat_axis=0, tiled=True)


def local(
    node_feats, batch_deg, batch_nbrs, halo_nbrs, halo_len, halo_rows, halo_deg,
    feat_table, emb_table, grad_table, weight_one, weight_two, grad_out,
):
    bdeg = batch_deg.reshape(1, NB)
    hdeg = halo_deg.reshape(1, NH)
    asked = exchange(halo_rows.reshape(128, 1, 4))
    h, gs, p = halo_call(halo_nbrs.T, halo_len.reshape(1, NB), bdeg, hdeg, grad_out)
    send = pick_call(asked, feat_table, emb_table, grad_table, p)
    recv = exchange(send)
    c, cf, sp, bp = batch_call(batch_nbrs.T, bdeg, node_feats, gs, weight_two)
    hid, grads = main_call(recv, h, cf, sp, bp, p, weight_one, weight_two, bdeg, hdeg)
    shares = exchange(grads)
    half = out_call(0, recv, c, h, hid, weight_two, bdeg, hdeg)
    shares, half = lax.optimization_barrier((shares, half))
    sums = exchange(sum_call(shares))
    out_embed = out_call(1, recv, c, h, hid, weight_two, bdeg, hdeg, half)
    halo_grad = tail_call(asked, recv)
    grad_one, grad_two = final_call(sums)
    return out_embed, halo_grad, grad_one, grad_two


def solution(mesh):
    rows = P(AXES, None)
    flat = P(AXES)
    return jax.shard_map(
        local,
        mesh=mesh,
        in_specs=(
            rows, flat, rows, rows, flat, flat, flat, rows, rows, rows, P(), P(), rows,
        ),
        out_specs=(rows, rows, P(), P()),
        check_vma=False,
    )
```

```python
import jax
import jax.numpy as jnp
from jax import lax
from jax.experimental import pallas as pl
from jax.experimental.pallas import tpu as pltpu
from jax.sharding import PartitionSpec as P

BF = jnp.bfloat16
F32 = jnp.float32
AXES = ("dp", "mp")
NB = 2048
NH = 512
HID = 512
FEAT = 128
STEP = 512


def hbm_spec():
    return pl.BlockSpec(memory_space=pltpu.HBM)


def vmem_spec():
    return pl.BlockSpec(memory_space=pltpu.VMEM)


def held(*shape, dtype=BF):
    return pltpu.VMEM(shape, dtype)


def keep(x):
    return pltpu.with_memory_space_constraint(x, pltpu.VMEM)


def leave(x):
    return pltpu.with_memory_space_constraint(x, pltpu.HBM)


def limit(mib):
    return pltpu.CompilerParams(vmem_limit_bytes=mib * 1024 * 1024)


def dot(left, right):
    return jnp.dot(left, right, preferred_element_type=F32)


def dot_t(left, right):
    return lax.dot_general(left, right, (((1,), (1,)), ((), ())), preferred_element_type=F32)


def dot_tl(left, right):
    return lax.dot_general(left, right, (((0,), (0,)), ((), ())), preferred_element_type=F32)


def columns(row):
    n = row.shape[1]
    return jnp.concatenate(
        [jnp.broadcast_to(row[:, s : s + 128], (128, 128)).T for s in range(0, n, 128)], axis=0
    )


def scale_rows(x, col):
    reps = x.shape[1] // 128
    return x * (jnp.tile(col, (1, reps)) if reps > 1 else col)


def count_tiles(dst_ref, nbrs, rows0, n_rows):
    times = jnp.ones(nbrs.shape, jnp.int32)
    for k in range(1, 8):
        times = times + (nbrs == pltpu.roll(nbrs, k, 0)).astype(jnp.int32)
    times = times.astype(F32)
    zero = jnp.zeros((16, 128), BF)
    sub = lax.broadcasted_iota(jnp.int32, (16, 128), 0)
    for c in range(0, nbrs.shape[1], 128):
        idx = [
            jnp.broadcast_to(nbrs[k : k + 1, c : c + 128], (16, 128)).astype(jnp.int16)
            for k in range(8)
        ]
        val = [jnp.broadcast_to(times[k : k + 1, c : c + 128], (16, 128)).astype(BF) for k in range(8)]

        def group(t, _):
            base = pl.multiple_of(t * 128, 128)
            first = (sub + (base + rows0)).astype(jnp.int16)
            for r in range(0, 128, 16):
                here = first + jnp.int16(r)
                acc = zero
                for k in range(8):
                    acc = jnp.where(idx[k] == here, val[k], acc)
                dst_ref[pl.ds(base + r, 16), c : c + 128] = acc
            return 0

        lax.fori_loop(0, n_rows // 128, group, 0)


def halo_kernel(
    hn_ref, hl_ref, bdeg_ref, hdeg_ref, g_hbm, h_hbm, gs_hbm, p_ref, g_ref, h_ref, gs_ref, sems
):
    copy_in = pltpu.make_async_copy(g_hbm, g_ref, sems.at[0])
    copy_in.start()
    nbrs = hn_ref[...]
    slot = lax.broadcasted_iota(jnp.int32, nbrs.shape, 0)
    nbrs = jnp.where(slot < hl_ref[...], nbrs, -1)
    count_tiles(h_ref, nbrs, 0, NH)
    copy_h = pltpu.make_async_copy(h_ref, h_hbm, sems.at[1])
    copy_h.start()
    inv = columns(lax.rsqrt(bdeg_ref[...].astype(F32)))
    inv_h = columns(lax.rsqrt(hdeg_ref[...].astype(F32)))
    copy_in.wait()
    for s in range(0, NB, STEP):
        gs = scale_rows(g_ref[s : s + STEP, :].astype(F32), inv[s : s + STEP])
        gs_ref[s : s + STEP, :] = gs.astype(BF)
    copy_gs = pltpu.make_async_copy(gs_ref, gs_hbm, sems.at[2])
    copy_gs.start()
    p_ref[...] = scale_rows(dot(h_ref[...], gs_ref[...]), inv_h).astype(BF)
    copy_h.wait()
    copy_gs.wait()


def halo_call(hn, hl, bdeg, hdeg, g):
    return pl.pallas_call(
        halo_kernel,
        in_specs=[vmem_spec()] * 4 + [hbm_spec()],
        out_specs=[hbm_spec(), hbm_spec(), vmem_spec()],
        out_shape=(
            pltpu.HBM((NH, NB), BF),
            pltpu.HBM((NB, HID), BF),
            held(NH, HID),
        ),
        scratch_shapes=[
            pltpu.VMEM((NB, HID), BF),
            pltpu.VMEM((NH, NB), BF),
            pltpu.VMEM((NB, HID), BF),
            pltpu.SemaphoreType.DMA((3,)),
        ],
        compiler_params=limit(58),
        name="halo_part",
    )(hn, hl, bdeg, hdeg, leave(g))


def rows_of(ref, lo, hi):
    return ref[:, :, lo:hi].reshape(NH, hi - lo)


def chunks_of(x):
    return x.astype(BF).reshape(x.shape[0] // 4, 4, x.shape[1])


def selector(ask_ref, s_ref):
    a = ask_ref[...].reshape(64, 2, 1, 4)
    sub = lax.broadcasted_iota(jnp.int32, (64, 8, 4), 1)
    lane = lax.broadcasted_iota(jnp.int32, (64, 8, 4), 2)
    mine = jnp.where(
        sub < 4, jnp.broadcast_to(a[:, 0], (64, 8, 4)), jnp.broadcast_to(a[:, 1], (64, 8, 4))
    )
    mine = jnp.where(lane == (sub & 3), mine & (NB - 1), 0)
    col = jnp.sum(mine.astype(F32), axis=2, keepdims=True).reshape(512, 1).astype(jnp.int32)
    colb = jnp.broadcast_to(col, (512, 128)).reshape(64, 8, 128)
    lanes = lax.broadcasted_iota(jnp.int32, (1, 8, 128), 2)
    for c in range(0, NB, 128):
        s_ref[:, c : c + 128] = jnp.where(colb == lanes + c, 1.0, 0.0).reshape(512, 128).astype(BF)


def pick_kernel(
    ask_ref, x_hbm, e_ref, v_hbm, p_ref, out_hbm, s_ref, x_ref, v_ref, out_ref, sems
):
    copies = [
        pltpu.make_async_copy(src, dst, sems.at[n])
        for n, (src, dst) in enumerate(((v_hbm, v_ref), (x_hbm, x_ref)))
    ]
    for copy in copies:
        copy.start()
    def send(lo, hi, n):
        at = (slice(None), slice(None), slice(lo, hi))
        sends.append(pltpu.make_async_copy(out_ref.at[at], out_hbm.at[at], sems.at[n]))
        sends[-1].start()

    sends = []
    out_ref[:, :, 1152:1664] = chunks_of(p_ref[...])
    send(1152, 1664, 3)
    selector(ask_ref, s_ref)
    s = s_ref[...]
    for n, (lo, hi, src) in enumerate(((128, 640, e_ref), (640, 1152, v_ref), (0, 128, x_ref))):
        if n:
            copies[n - 1].wait()
        out_ref[:, :, lo:hi] = chunks_of(dot(s, src[...]))
        send(lo, hi, 4 + n)
    for copy in sends:
        copy.wait()


def pick_call(asked, x, e, v, p):
    return pl.pallas_call(
        pick_kernel,
        in_specs=[vmem_spec(), hbm_spec(), vmem_spec(), hbm_spec(), vmem_spec()],
        out_specs=hbm_spec(),
        out_shape=pltpu.HBM((128, 4, 1664), BF),
        scratch_shapes=[
            pltpu.VMEM((NH, NB), BF),
            pltpu.VMEM((NB, FEAT), BF),
            pltpu.VMEM((NB, HID), BF),
            pltpu.VMEM((128, 4, 1664), BF),
            pltpu.SemaphoreType.DMA((7,)),
        ],
        compiler_params=limit(58),
        name="pick_rows",
    )(keep(asked), leave(x), keep(e), leave(v), keep(p))


def batch_kernel(
    nb_ref, bdeg_ref, f_ref, gs_ref, w2_ref, c_hbm, cf_ref, sp_hbm, bp_hbm,
    fs_ref, c_ref, sp_ref, bp_ref, sems,
):
    col = columns(lax.rsqrt(bdeg_ref[...].astype(F32)))
    fs_ref[...] = (f_ref[...].astype(F32) * col).astype(BF)
    eye = (
        lax.broadcasted_iota(jnp.int32, (128, 128), 0)
        == lax.broadcasted_iota(jnp.int32, (128, 128), 1)
    ).astype(F32).astype(BF)
    count_tiles(c_ref, nb_ref[...], 0, NB)
    for r in range(0, NB, 128):
        c_ref[r : r + 128, r : r + 128] = c_ref[r : r + 128, r : r + 128] + eye
    copies = [pltpu.make_async_copy(c_ref, c_hbm, sems.at[0])]
    copies[0].start()
    for n, r in enumerate(range(0, NB, STEP)):
        at = slice(r, r + STEP)
        spread = dot(c_ref[at, :], gs_ref[...]).astype(BF)
        sp_ref[at, :] = spread
        bp_ref[at, :] = dot_t(spread, w2_ref[...])
        for m, (src, dst) in enumerate(((sp_ref, sp_hbm), (bp_ref, bp_hbm))):
            copies.append(pltpu.make_async_copy(src.at[at], dst.at[at], sems.at[1 + 2 * n + m]))
            copies[-1].start()
        cf_ref[at, :] = dot_tl(c_ref[:, at], fs_ref[...])
    for copy in copies:
        copy.wait()


def batch_call(nb, bdeg, f, gs, w2):
    return pl.pallas_call(
        batch_kernel,
        in_specs=[vmem_spec()] * 5,
        out_specs=[hbm_spec(), vmem_spec(), hbm_spec(), hbm_spec()],
        out_shape=(
            pltpu.HBM((NB, NB), BF),
            pltpu.HBM((NB, FEAT), F32),
            pltpu.HBM((NB, HID), BF),
            pltpu.HBM((NB, HID), F32),
        ),
        scratch_shapes=[
            pltpu.VMEM((NB, FEAT), BF),
            pltpu.VMEM((NB, NB), BF),
            pltpu.VMEM((NB, HID), BF),
            pltpu.VMEM((NB, HID), F32),
            pltpu.SemaphoreType.DMA((9,)),
        ],
        compiler_params=limit(58),
        name="batch_part",
    )(nb, bdeg, f, gs, w2)


def main_kernel(
    r_ref, h_hbm, cf_hbm, sp_hbm, bp_hbm, p_ref, w1_hbm, w2_hbm, bdeg_hbm, hdeg_hbm,
    hid_hbm, grads_ref,
    h_ref, cf_ref, sp_ref, bp_ref, w1_ref, w2_ref, bdeg_ref, hdeg_ref,
    hid_ref, mix_ref, g1_ref, g2_ref, sems,
):
    first = (
        (hdeg_hbm, hdeg_ref), (w2_hbm, w2_ref), (bdeg_hbm, bdeg_ref),
        (h_hbm, h_ref), (cf_hbm, cf_ref), (w1_hbm, w1_ref),
    )
    copies = [pltpu.make_async_copy(src, dst, sems.at[n]) for n, (src, dst) in enumerate(first)]
    for copy in copies:
        copy.start()
    bp_copies = [
        pltpu.make_async_copy(bp_hbm.at[s : s + STEP], bp_ref.at[s : s + STEP], sems.at[6 + s // STEP])
        for s in range(0, NB, STEP)
    ]
    sp_copy = pltpu.make_async_copy(sp_hbm, sp_ref, sems.at[10])
    g2_ref[...] = dot_tl(rows_of(r_ref, 128, 640), p_ref[...])
    copies[0].wait()
    col_h = columns(lax.rsqrt(hdeg_ref[...].astype(F32)))
    mix_ref[:, 512:640] = (rows_of(r_ref, 0, 128).astype(F32) * col_h).astype(BF)
    copies[1].wait()
    mix_ref[:, 0:512] = scale_rows(dot_t(rows_of(r_ref, 640, 1152), w2_ref[...]), col_h).astype(BF)
    copies[2].wait()
    inv = columns(lax.rsqrt(bdeg_ref[...].astype(F32)))
    for copy in copies[3:]:
        copy.wait()
    for copy in bp_copies:
        copy.start()
    sp_copy.start()
    outs = []
    for n, s in enumerate(range(0, NB, STEP)):
        at = slice(s, s + STEP)
        half = 0.5 * inv[at]
        half_sq = half * inv[at]
        h = h_ref[:, at]
        u1 = (cf_ref[at, :] + dot_tl(h, mix_ref[:, 512:640])).astype(BF)
        z = dot(u1, w1_ref[...])
        zh = scale_rows(z, half)
        t = jnp.tanh(zh)
        w = scale_rows(1.0 + t, half_sq)
        hid_ref[at, :] = (z * w).astype(BF)
        outs.append(pltpu.make_async_copy(hid_ref.at[at], hid_hbm.at[at], sems.at[11 + n]))
        outs[-1].start()
        bp_copies[n].wait()
        d_pre = ((bp_ref[at, :] + dot_tl(h, mix_ref[:, 0:512])) * (w * (1.0 + zh * (1.0 - t)))).astype(BF)
        g1 = dot_tl(u1, d_pre)
        if n == 0:
            g1_ref[...] = g1
        else:
            g1_ref[...] += g1
    sp_copy.wait()
    g2_ref[...] += dot_tl(hid_ref[...], sp_ref[...])
    grads_ref[:, :, 0:512] = chunks_of(g2_ref[...])
    for q in range(4):
        part = g1_ref[:, 128 * q : 128 * q + 128]
        grads_ref[32 * q : 32 * q + 32, :, 512:640] = chunks_of(part)
    for copy in outs:
        copy.wait()


def main_call(recv, h, cf, sp, bp, p, w1, w2, bdeg, hdeg):
    return pl.pallas_call(
        main_kernel,
        in_specs=[vmem_spec()] + [hbm_spec()] * 4 + [vmem_spec()] + [hbm_spec()] * 4,
        out_specs=[hbm_spec(), vmem_spec()],
        out_shape=(pltpu.HBM((NB, HID), BF), jax.ShapeDtypeStruct((128, 4, 640), BF)),
        scratch_shapes=[
            pltpu.VMEM((NH, NB), BF),
            pltpu.VMEM((NB, FEAT), F32),
            pltpu.VMEM((NB, HID), BF),
            pltpu.VMEM((NB, HID), F32),
            pltpu.VMEM((FEAT, HID), BF),
            pltpu.VMEM((HID, HID), BF),
            pltpu.VMEM((1, NB), jnp.int32),
            pltpu.VMEM((1, NH), jnp.int32),
            pltpu.VMEM((NB, HID), BF),
            pltpu.VMEM((NH, HID + FEAT), BF),
            pltpu.VMEM((FEAT, HID), F32),
            pltpu.VMEM((HID, HID), F32),
            pltpu.SemaphoreType.DMA((15,)),
        ],
        compiler_params=limit(58),
        name="main_part",
    )(keep(recv), leave(h), leave(cf), leave(sp), leave(bp), keep(p), leave(w1), leave(w2), leave(bdeg), leave(hdeg))


def out_kernel(half, refs):
    r_ref, c_hbm, h_hbm, hid_ref, w2_ref, bdeg_ref, hdeg_ref = refs[:7]
    out_hbm, c_ref, h_ref, he_ref, out_ref, sems = refs[-6:]
    at = slice(half * NB // 2, (half + 1) * NB // 2)
    ins = [
        pltpu.make_async_copy(c_hbm.at[:, at], c_ref, sems.at[0]),
        pltpu.make_async_copy(h_hbm.at[:, at], h_ref, sems.at[1]),
    ]
    for copy in ins:
        copy.start()
    inv = columns(lax.rsqrt(bdeg_ref[:, at].astype(F32)))
    col_h = columns(lax.rsqrt(hdeg_ref[...].astype(F32)))
    he_ref[...] = scale_rows(rows_of(r_ref, 128, 640).astype(F32), col_h).astype(BF)
    for copy in ins:
        copy.wait()
    outs = []
    for n, s in enumerate(range(0, NB // 2, STEP)):
        here = slice(s, s + STEP)
        there = slice(at.start + s, at.start + s + STEP)
        u = dot_tl(c_ref[:, here], hid_ref[...]) + dot_tl(h_ref[:, here], he_ref[...])
        out_ref[here] = scale_rows(dot(u.astype(BF), w2_ref[...]), inv[here]).astype(BF)
        outs.append(pltpu.make_async_copy(out_ref.at[here], out_hbm.at[there], sems.at[2 + n]))
        outs[-1].start()
    for copy in outs:
        copy.wait()


def out_call(half, recv, c, h, hid, w2, bdeg, hdeg, *first):
    return pl.pallas_call(
        lambda *refs: out_kernel(half, refs),
        in_specs=[vmem_spec(), hbm_spec(), hbm_spec()] + [vmem_spec()] * 4 + [hbm_spec()] * len(first),
        out_specs=hbm_spec(),
        out_shape=pltpu.HBM((NB, HID), BF),
        input_output_aliases={7: 0} if first else {},
        scratch_shapes=[
            pltpu.VMEM((NB, NB // 2), BF),
            pltpu.VMEM((NH, NB // 2), BF),
            pltpu.VMEM((NH, HID), BF),
            pltpu.VMEM((NB // 2, HID), BF),
            pltpu.SemaphoreType.DMA((4,)),
        ],
        compiler_params=limit(58),
        name=f"out_part_{half}",
    )(keep(recv), leave(c), leave(h), hid, w2, bdeg, hdeg, *first)


def tail_kernel(ask_ref, r_ref, hg_hbm, s_ref, pa_ref, hg_ref, sems):
    selector(ask_ref, s_ref)
    pa_ref[...] = rows_of(r_ref, 1152, 1664)
    copies = []
    for n, r in enumerate(range(0, NB, STEP)):
        at = slice(r, r + STEP)
        hg_ref[at] = dot_tl(s_ref[:, at], pa_ref[...]).astype(BF)
        copies.append(pltpu.make_async_copy(hg_ref.at[at], hg_hbm.at[at], sems.at[n]))
        copies[-1].start()
    for copy in copies:
        copy.wait()


def tail_call(asked, recv):
    return pl.pallas_call(
        tail_kernel,
        in_specs=[vmem_spec()] * 2,
        out_specs=hbm_spec(),
        out_shape=jax.ShapeDtypeStruct((NB, HID), BF),
        scratch_shapes=[
            pltpu.VMEM((NH, NB), BF),
            pltpu.VMEM((NH, HID), BF),
            pltpu.VMEM((NB, HID), BF),
            pltpu.SemaphoreType.DMA((4,)),
        ],
        compiler_params=limit(58),
        name="tail_part",
    )(keep(asked), keep(recv))


def sum_kernel(x_ref, o_ref):
    total = jnp.sum(x_ref[...].astype(F32), axis=0)
    o_ref[...] = jnp.broadcast_to(total.astype(BF)[None], (128, 4, 640))


def sum_call(x):
    return pl.pallas_call(
        sum_kernel,
        in_specs=[vmem_spec()],
        out_specs=vmem_spec(),
        out_shape=jax.ShapeDtypeStruct((128, 4, 640), BF),
        name="sum_part",
    )(keep(x))


def final_kernel(x_ref, g1_ref, g2_ref):
    factor = 1.0 / 512.0
    g2_ref[...] = rows_of(x_ref, 0, 512).astype(F32) * factor
    for q in range(4):
        part = x_ref[32 * q : 32 * q + 32, :, 512:640].reshape(128, 128)
        g1_ref[:, 128 * q : 128 * q + 128] = part.astype(F32) * factor


def final_call(x):
    return pl.pallas_call(
        final_kernel,
        in_specs=[vmem_spec()],
        out_specs=[vmem_spec()] * 2,
        out_shape=(
            jax.ShapeDtypeStruct((FEAT, HID), F32),
            jax.ShapeDtypeStruct((HID, HID), F32),
        ),
        name="final_part",
    )(keep(x))


def exchange(x):
    return lax.all_to_all(x, AXES, split_axis=0, concat_axis=0, tiled=True)


def local(
    node_feats, batch_deg, batch_nbrs, halo_nbrs, halo_len, halo_rows, halo_deg,
    feat_table, emb_table, grad_table, weight_one, weight_two, grad_out,
):
    bdeg = batch_deg.reshape(1, NB)
    hdeg = halo_deg.reshape(1, NH)
    asked = exchange(halo_rows.reshape(128, 1, 4))
    h, gs, p = halo_call(halo_nbrs.T, halo_len.reshape(1, NB), bdeg, hdeg, grad_out)
    send = pick_call(asked, feat_table, emb_table, grad_table, p)
    recv = exchange(send)
    c, cf, sp, bp = batch_call(batch_nbrs.T, bdeg, node_feats, gs, weight_two)
    hid, grads = main_call(recv, h, cf, sp, bp, p, weight_one, weight_two, bdeg, hdeg)
    shares = exchange(grads)
    half = out_call(0, recv, c, h, hid, weight_two, bdeg, hdeg)
    shares, half = lax.optimization_barrier((shares, half))
    sums = exchange(sum_call(shares))
    out_embed = out_call(1, recv, c, h, hid, weight_two, bdeg, hdeg, half)
    halo_grad = tail_call(asked, recv)
    grad_one, grad_two = final_call(sums)
    return out_embed, halo_grad, grad_one, grad_two


def solution(mesh):
    rows = P(AXES, None)
    flat = P(AXES)
    return jax.shard_map(
        local,
        mesh=mesh,
        in_specs=(
            rows, flat, rows, rows, flat, flat, flat, rows, rows, rows, P(), P(), rows,
        ),
        out_specs=(rows, rows, P(), P()),
        check_vma=False,
    )
```

```python
import jax
import jax.numpy as jnp
from jax import lax
from jax.experimental import pallas as pl
from jax.experimental.pallas import tpu as pltpu
from jax.sharding import PartitionSpec as P

BF = jnp.bfloat16
F32 = jnp.float32
AXES = ("dp", "mp")
NB = 2048
NH = 512
HID = 512
FEAT = 128
STEP = 512


def hbm_spec():
    return pl.BlockSpec(memory_space=pltpu.HBM)


def vmem_spec():
    return pl.BlockSpec(memory_space=pltpu.VMEM)


def held(*shape, dtype=BF):
    return pltpu.VMEM(shape, dtype)


def keep(x):
    return pltpu.with_memory_space_constraint(x, pltpu.VMEM)


def leave(x):
    return pltpu.with_memory_space_constraint(x, pltpu.HBM)


def limit(mib):
    return pltpu.CompilerParams(vmem_limit_bytes=mib * 1024 * 1024)


def dot(left, right):
    return jnp.dot(left, right, preferred_element_type=F32)


def dot_t(left, right):
    return lax.dot_general(left, right, (((1,), (1,)), ((), ())), preferred_element_type=F32)


def dot_tl(left, right):
    return lax.dot_general(left, right, (((0,), (0,)), ((), ())), preferred_element_type=F32)


def columns(row):
    n = row.shape[1]
    return jnp.concatenate(
        [jnp.broadcast_to(row[:, s : s + 128], (128, 128)).T for s in range(0, n, 128)], axis=0
    )


def scale_rows(x, col):
    reps = x.shape[1] // 128
    return x * (jnp.tile(col, (1, reps)) if reps > 1 else col)


def count_tiles(dst_ref, nbrs, rows0, n_rows, weight=1.0):
    times = jnp.ones(nbrs.shape, jnp.int32)
    for k in range(1, 8):
        times = times + (nbrs == pltpu.roll(nbrs, k, 0)).astype(jnp.int32)
    times = times.astype(F32) * weight
    zero = jnp.zeros((16, 128), BF)
    sub = lax.broadcasted_iota(jnp.int32, (16, 128), 0)
    for c in range(0, nbrs.shape[1], 128):
        idx = [
            jnp.broadcast_to(nbrs[k : k + 1, c : c + 128], (16, 128)).astype(jnp.int16)
            for k in range(8)
        ]
        val = [jnp.broadcast_to(times[k : k + 1, c : c + 128], (16, 128)).astype(BF) for k in range(8)]

        def group(t, _):
            base = pl.multiple_of(t * 128, 128)
            first = (sub + (base + rows0)).astype(jnp.int16)
            for r in range(0, 128, 16):
                here = first + jnp.int16(r)
                acc = zero
                for k in range(8):
                    acc = jnp.where(idx[k] == here, val[k], acc)
                dst_ref[pl.ds(base + r, 16), c : c + 128] = acc
            return 0

        lax.fori_loop(0, n_rows // 128, group, 0)


def halo_kernel(hn_ref, hl_ref, bdeg_ref, hdeg_ref, g_hbm, h_hbm, p_ref, g_ref, h_ref, sems):
    copy_in = pltpu.make_async_copy(g_hbm, g_ref, sems.at[0])
    copy_in.start()
    nbrs = hn_ref[...]
    slot = lax.broadcasted_iota(jnp.int32, nbrs.shape, 0)
    nbrs = jnp.where(slot < hl_ref[...], nbrs, -1)
    count_tiles(h_ref, nbrs, 0, NH, lax.rsqrt(bdeg_ref[...].astype(F32)))
    copy_h = pltpu.make_async_copy(h_ref, h_hbm, sems.at[1])
    copy_h.start()
    inv_h = columns(lax.rsqrt(hdeg_ref[...].astype(F32)))
    copy_in.wait()
    p_ref[...] = scale_rows(dot(h_ref[...], g_ref[...]), inv_h).astype(BF)
    copy_h.wait()


def halo_call(hn, hl, bdeg, hdeg, g):
    return pl.pallas_call(
        halo_kernel,
        in_specs=[vmem_spec()] * 4 + [hbm_spec()],
        out_specs=[hbm_spec(), vmem_spec()],
        out_shape=(pltpu.HBM((NH, NB), BF), held(NH, HID)),
        scratch_shapes=[
            pltpu.VMEM((NB, HID), BF),
            pltpu.VMEM((NH, NB), BF),
            pltpu.SemaphoreType.DMA((2,)),
        ],
        compiler_params=limit(58),
        name="halo_part",
    )(hn, hl, bdeg, hdeg, leave(g))


def rows_of(ref, lo, hi):
    return ref[:, :, lo:hi].reshape(NH, hi - lo)


def chunks_of(x):
    return x.astype(BF).reshape(x.shape[0] // 4, 4, x.shape[1])


def selector(ask_ref, s_ref):
    a = ask_ref[...].reshape(64, 2, 1, 4)
    sub = lax.broadcasted_iota(jnp.int32, (64, 8, 4), 1)
    lane = lax.broadcasted_iota(jnp.int32, (64, 8, 4), 2)
    mine = jnp.where(
        sub < 4, jnp.broadcast_to(a[:, 0], (64, 8, 4)), jnp.broadcast_to(a[:, 1], (64, 8, 4))
    )
    mine = jnp.where(lane == (sub & 3), mine & (NB - 1), 0)
    col = jnp.sum(mine.astype(F32), axis=2, keepdims=True).reshape(512, 1).astype(jnp.int32)
    colb = jnp.broadcast_to(col, (512, 128)).reshape(64, 8, 128)
    lanes = lax.broadcasted_iota(jnp.int32, (1, 8, 128), 2)
    for c in range(0, NB, 128):
        s_ref[:, c : c + 128] = jnp.where(colb == lanes + c, 1.0, 0.0).reshape(512, 128).astype(BF)


def pick_kernel(
    ask_ref, x_hbm, e_ref, v_hbm, p_ref, out_hbm, s_ref, x_ref, v_ref, out_ref, sems
):
    copies = [
        pltpu.make_async_copy(src, dst, sems.at[n])
        for n, (src, dst) in enumerate(((v_hbm, v_ref), (x_hbm, x_ref)))
    ]
    for copy in copies:
        copy.start()
    def send(lo, hi, n):
        at = (slice(None), slice(None), slice(lo, hi))
        sends.append(pltpu.make_async_copy(out_ref.at[at], out_hbm.at[at], sems.at[n]))
        sends[-1].start()

    sends = []
    out_ref[:, :, 1152:1664] = chunks_of(p_ref[...])
    send(1152, 1664, 3)
    selector(ask_ref, s_ref)
    s = s_ref[...]
    for n, (lo, hi, src) in enumerate(((128, 640, e_ref), (640, 1152, v_ref), (0, 128, x_ref))):
        if n:
            copies[n - 1].wait()
        out_ref[:, :, lo:hi] = chunks_of(dot(s, src[...]))
        send(lo, hi, 4 + n)
    for copy in sends:
        copy.wait()


def pick_call(asked, x, e, v, p):
    return pl.pallas_call(
        pick_kernel,
        in_specs=[vmem_spec(), hbm_spec(), vmem_spec(), hbm_spec(), vmem_spec()],
        out_specs=hbm_spec(),
        out_shape=pltpu.HBM((128, 4, 1664), BF),
        scratch_shapes=[
            pltpu.VMEM((NH, NB), BF),
            pltpu.VMEM((NB, FEAT), BF),
            pltpu.VMEM((NB, HID), BF),
            pltpu.VMEM((128, 4, 1664), BF),
            pltpu.SemaphoreType.DMA((7,)),
        ],
        compiler_params=limit(58),
        name="pick_rows",
    )(keep(asked), leave(x), keep(e), leave(v), keep(p))


def batch_kernel(
    nb_ref, bdeg_ref, f_ref, g_hbm, w2_ref, c_hbm, cf_ref, sp_hbm, bp_hbm,
    fs_ref, g_ref, gs_ref, c_ref, sp_ref, bp_ref, sems,
):
    copy_in = pltpu.make_async_copy(g_hbm, g_ref, sems.at[9])
    copy_in.start()
    col = columns(lax.rsqrt(bdeg_ref[...].astype(F32)))
    fs_ref[...] = (f_ref[...].astype(F32) * col).astype(BF)
    eye = (
        lax.broadcasted_iota(jnp.int32, (128, 128), 0)
        == lax.broadcasted_iota(jnp.int32, (128, 128), 1)
    ).astype(F32).astype(BF)
    count_tiles(c_ref, nb_ref[...], 0, NB)
    for r in range(0, NB, 128):
        c_ref[r : r + 128, r : r + 128] = c_ref[r : r + 128, r : r + 128] + eye
    copies = [pltpu.make_async_copy(c_ref, c_hbm, sems.at[0])]
    copies[0].start()
    copy_in.wait()
    for s in range(0, NB, STEP):
        gs = scale_rows(g_ref[s : s + STEP, :].astype(F32), col[s : s + STEP])
        gs_ref[s : s + STEP, :] = gs.astype(BF)
    for n, r in enumerate(range(0, NB, STEP)):
        at = slice(r, r + STEP)
        spread = dot(c_ref[at, :], gs_ref[...]).astype(BF)
        sp_ref[at, :] = spread
        bp_ref[at, :] = scale_rows(dot_t(spread, w2_ref[...]), col[at])
        for m, (src, dst) in enumerate(((sp_ref, sp_hbm), (bp_ref, bp_hbm))):
            copies.append(pltpu.make_async_copy(src.at[at], dst.at[at], sems.at[1 + 2 * n + m]))
            copies[-1].start()
        cf_ref[at, :] = dot_tl(c_ref[:, at], fs_ref[...]) * col[at]
    for copy in copies:
        copy.wait()


def batch_call(nb, bdeg, f, g, w2):
    return pl.pallas_call(
        batch_kernel,
        in_specs=[vmem_spec()] * 3 + [hbm_spec(), vmem_spec()],
        out_specs=[hbm_spec(), vmem_spec(), hbm_spec(), hbm_spec()],
        out_shape=(
            pltpu.HBM((NB, NB), BF),
            pltpu.HBM((NB, FEAT), F32),
            pltpu.HBM((NB, HID), BF),
            pltpu.HBM((NB, HID), F32),
        ),
        scratch_shapes=[
            pltpu.VMEM((NB, FEAT), BF),
            pltpu.VMEM((NB, HID), BF),
            pltpu.VMEM((NB, HID), BF),
            pltpu.VMEM((NB, NB), BF),
            pltpu.VMEM((NB, HID), BF),
            pltpu.VMEM((NB, HID), F32),
            pltpu.SemaphoreType.DMA((10,)),
        ],
        compiler_params=limit(58),
        name="batch_part",
    )(nb, bdeg, f, leave(g), w2)


def main_kernel(
    r_ref, h_hbm, cf_hbm, sp_hbm, bp_hbm, p_ref, w1_hbm, w2_hbm, bdeg_hbm, hdeg_hbm,
    hid_hbm, grads_ref,
    h_ref, cf_ref, sp_ref, bp_ref, w1_ref, w2_ref, bdeg_ref, hdeg_ref,
    hid_ref, mix_ref, g1_ref, g2_ref, sems,
):
    first = ((hdeg_hbm, hdeg_ref), (w2_hbm, w2_ref), (bdeg_hbm, bdeg_ref), (w1_hbm, w1_ref))
    copies = [pltpu.make_async_copy(src, dst, sems.at[n]) for n, (src, dst) in enumerate(first)]
    for copy in copies:
        copy.start()
    blocks = []
    for n, s in enumerate(range(0, NB, STEP)):
        at = slice(s, s + STEP)
        blocks.append([
            pltpu.make_async_copy(h_hbm.at[:, at], h_ref.at[:, at], sems.at[4 + 3 * n]),
            pltpu.make_async_copy(cf_hbm.at[at], cf_ref.at[at], sems.at[5 + 3 * n]),
            pltpu.make_async_copy(bp_hbm.at[at], bp_ref.at[at], sems.at[6 + 3 * n]),
        ])
    sp_copy = pltpu.make_async_copy(sp_hbm, sp_ref, sems.at[16])
    for copy in blocks[0]:
        copy.start()
    g2_ref[...] = dot_tl(rows_of(r_ref, 128, 640), p_ref[...])
    copies[0].wait()
    col_h = columns(lax.rsqrt(hdeg_ref[...].astype(F32)))
    mix_ref[:, 512:640] = (rows_of(r_ref, 0, 128).astype(F32) * col_h).astype(BF)
    copies[1].wait()
    mix_ref[:, 0:512] = scale_rows(dot_t(rows_of(r_ref, 640, 1152), w2_ref[...]), col_h).astype(BF)
    for block in blocks[1:]:
        for copy in block:
            copy.start()
    sp_copy.start()
    copies[2].wait()
    inv = columns(lax.rsqrt(bdeg_ref[...].astype(F32)))
    copies[3].wait()
    outs = []
    for n, s in enumerate(range(0, NB, STEP)):
        at = slice(s, s + STEP)
        blocks[n][0].wait()
        blocks[n][1].wait()
        h = h_ref[:, at]
        u1 = (cf_ref[at, :] + dot_tl(h, mix_ref[:, 512:640])).astype(BF)
        zh = 0.5 * dot(u1, w1_ref[...])
        t = jnp.tanh(zh)
        hid_ref[at, :] = (zh * scale_rows(1.0 + t, inv[at])).astype(BF)
        outs.append(pltpu.make_async_copy(hid_ref.at[at], hid_hbm.at[at], sems.at[17 + n]))
        outs[-1].start()
        slope = (0.5 + 0.5 * t) * (1.0 + zh * (1.0 - t))
        blocks[n][2].wait()
        d_pre = ((bp_ref[at, :] + dot_tl(h, mix_ref[:, 0:512])) * slope).astype(BF)
        g1 = dot_tl(u1, d_pre)
        if n == 0:
            g1_ref[...] = g1
        else:
            g1_ref[...] += g1
    sp_copy.wait()
    g2_ref[...] += dot_tl(hid_ref[...], sp_ref[...])
    grads_ref[:, :, 0:512] = chunks_of(g2_ref[...])
    for q in range(4):
        part = g1_ref[:, 128 * q : 128 * q + 128]
        grads_ref[32 * q : 32 * q + 32, :, 512:640] = chunks_of(part)
    for copy in outs:
        copy.wait()


def main_call(recv, h, cf, sp, bp, p, w1, w2, bdeg, hdeg):
    return pl.pallas_call(
        main_kernel,
        in_specs=[vmem_spec()] + [hbm_spec()] * 4 + [vmem_spec()] + [hbm_spec()] * 4,
        out_specs=[hbm_spec(), vmem_spec()],
        out_shape=(pltpu.HBM((NB, HID), BF), jax.ShapeDtypeStruct((128, 4, 640), BF)),
        scratch_shapes=[
            pltpu.VMEM((NH, NB), BF),
            pltpu.VMEM((NB, FEAT), F32),
            pltpu.VMEM((NB, HID), BF),
            pltpu.VMEM((NB, HID), F32),
            pltpu.VMEM((FEAT, HID), BF),
            pltpu.VMEM((HID, HID), BF),
            pltpu.VMEM((1, NB), jnp.int32),
            pltpu.VMEM((1, NH), jnp.int32),
            pltpu.VMEM((NB, HID), BF),
            pltpu.VMEM((NH, HID + FEAT), BF),
            pltpu.VMEM((FEAT, HID), F32),
            pltpu.VMEM((HID, HID), F32),
            pltpu.SemaphoreType.DMA((21,)),
        ],
        compiler_params=limit(58),
        name="main_part",
    )(keep(recv), leave(h), leave(cf), leave(sp), leave(bp), keep(p), leave(w1), leave(w2), leave(bdeg), leave(hdeg))


def out_kernel(half, refs):
    r_ref, c_hbm, h_hbm, hid_ref, w2_ref, bdeg_ref, hdeg_ref = refs[:7]
    out_hbm, c_ref, h_ref, he_ref, out_ref, sems = refs[-6:]
    at = slice(half * NB // 2, (half + 1) * NB // 2)
    ins = [
        pltpu.make_async_copy(c_hbm.at[:, at], c_ref, sems.at[0]),
        pltpu.make_async_copy(h_hbm.at[:, at], h_ref, sems.at[1]),
    ]
    for copy in ins:
        copy.start()
    inv = columns(lax.rsqrt(bdeg_ref[:, at].astype(F32)))
    col_h = columns(lax.rsqrt(hdeg_ref[...].astype(F32)))
    he_ref[...] = scale_rows(rows_of(r_ref, 128, 640).astype(F32), col_h).astype(BF)
    for copy in ins:
        copy.wait()
    outs = []
    for n, s in enumerate(range(0, NB // 2, STEP)):
        here = slice(s, s + STEP)
        there = slice(at.start + s, at.start + s + STEP)
        own = scale_rows(dot_tl(c_ref[:, here], hid_ref[...]), inv[here])
        u = (own + dot_tl(h_ref[:, here], he_ref[...])).astype(BF)
        out_ref[here] = dot(u, w2_ref[...]).astype(BF)
        outs.append(pltpu.make_async_copy(out_ref.at[here], out_hbm.at[there], sems.at[2 + n]))
        outs[-1].start()
    for copy in outs:
        copy.wait()


def out_call(half, recv, c, h, hid, w2, bdeg, hdeg, *first):
    return pl.pallas_call(
        lambda *refs: out_kernel(half, refs),
        in_specs=[vmem_spec(), hbm_spec(), hbm_spec()] + [vmem_spec()] * 4 + [hbm_spec()] * len(first),
        out_specs=hbm_spec(),
        out_shape=pltpu.HBM((NB, HID), BF),
        input_output_aliases={7: 0} if first else {},
        scratch_shapes=[
            pltpu.VMEM((NB, NB // 2), BF),
            pltpu.VMEM((NH, NB // 2), BF),
            pltpu.VMEM((NH, HID), BF),
            pltpu.VMEM((NB // 2, HID), BF),
            pltpu.SemaphoreType.DMA((4,)),
        ],
        compiler_params=limit(58),
        name=f"out_part_{half}",
    )(keep(recv), leave(c), leave(h), hid, w2, bdeg, hdeg, *first)


def tail_kernel(ask_ref, r_ref, hg_hbm, s_ref, pa_ref, hg_ref, sems):
    selector(ask_ref, s_ref)
    pa_ref[...] = rows_of(r_ref, 1152, 1664)
    copies = []
    for n, r in enumerate(range(0, NB, STEP)):
        at = slice(r, r + STEP)
        hg_ref[at] = dot_tl(s_ref[:, at], pa_ref[...]).astype(BF)
        copies.append(pltpu.make_async_copy(hg_ref.at[at], hg_hbm.at[at], sems.at[n]))
        copies[-1].start()
    for copy in copies:
        copy.wait()


def tail_call(asked, recv):
    return pl.pallas_call(
        tail_kernel,
        in_specs=[vmem_spec()] * 2,
        out_specs=hbm_spec(),
        out_shape=jax.ShapeDtypeStruct((NB, HID), BF),
        scratch_shapes=[
            pltpu.VMEM((NH, NB), BF),
            pltpu.VMEM((NH, HID), BF),
            pltpu.VMEM((NB, HID), BF),
            pltpu.SemaphoreType.DMA((4,)),
        ],
        compiler_params=limit(58),
        name="tail_part",
    )(keep(asked), keep(recv))


def sum_kernel(x_ref, o_ref):
    total = jnp.sum(x_ref[...].astype(F32), axis=0)
    o_ref[...] = jnp.broadcast_to(total.astype(BF)[None], (128, 4, 640))


def sum_call(x):
    return pl.pallas_call(
        sum_kernel,
        in_specs=[vmem_spec()],
        out_specs=vmem_spec(),
        out_shape=jax.ShapeDtypeStruct((128, 4, 640), BF),
        name="sum_part",
    )(keep(x))


def final_kernel(x_ref, g1_ref, g2_ref):
    factor = 1.0 / 512.0
    g2_ref[...] = rows_of(x_ref, 0, 512).astype(F32) * factor
    for q in range(4):
        part = x_ref[32 * q : 32 * q + 32, :, 512:640].reshape(128, 128)
        g1_ref[:, 128 * q : 128 * q + 128] = part.astype(F32) * factor


def final_call(x):
    return pl.pallas_call(
        final_kernel,
        in_specs=[vmem_spec()],
        out_specs=[vmem_spec()] * 2,
        out_shape=(
            jax.ShapeDtypeStruct((FEAT, HID), F32),
            jax.ShapeDtypeStruct((HID, HID), F32),
        ),
        name="final_part",
    )(keep(x))


def exchange(x):
    return lax.all_to_all(x, AXES, split_axis=0, concat_axis=0, tiled=True)


def local(
    node_feats, batch_deg, batch_nbrs, halo_nbrs, halo_len, halo_rows, halo_deg,
    feat_table, emb_table, grad_table, weight_one, weight_two, grad_out,
):
    bdeg = batch_deg.reshape(1, NB)
    hdeg = halo_deg.reshape(1, NH)
    asked = exchange(halo_rows.reshape(128, 1, 4))
    h, p = halo_call(halo_nbrs.T, halo_len.reshape(1, NB), bdeg, hdeg, grad_out)
    send = pick_call(asked, feat_table, emb_table, grad_table, p)
    recv = exchange(send)
    c, cf, sp, bp = batch_call(batch_nbrs.T, bdeg, node_feats, grad_out, weight_two)
    hid, grads = main_call(recv, h, cf, sp, bp, p, weight_one, weight_two, bdeg, hdeg)
    shares = exchange(grads)
    half = out_call(0, recv, c, h, hid, weight_two, bdeg, hdeg)
    shares, half = lax.optimization_barrier((shares, half))
    sums = exchange(sum_call(shares))
    out_embed = out_call(1, recv, c, h, hid, weight_two, bdeg, hdeg, half)
    halo_grad = tail_call(asked, recv)
    grad_one, grad_two = final_call(sums)
    return out_embed, halo_grad, grad_one, grad_two


def solution(mesh):
    rows = P(AXES, None)
    flat = P(AXES)
    return jax.shard_map(
        local,
        mesh=mesh,
        in_specs=(
            rows, flat, rows, rows, flat, flat, flat, rows, rows, rows, P(), P(), rows,
        ),
        out_specs=(rows, rows, P(), P()),
        check_vma=False,
    )
```

```python
import jax
import jax.numpy as jnp
from jax import lax
from jax.experimental import pallas as pl
from jax.experimental.pallas import tpu as pltpu
from jax.sharding import PartitionSpec as P

BF = jnp.bfloat16
F32 = jnp.float32
AXES = ("dp", "mp")
NB = 2048
NH = 512
HID = 512
FEAT = 128
STEP = 512


def hbm_spec():
    return pl.BlockSpec(memory_space=pltpu.HBM)


def vmem_spec():
    return pl.BlockSpec(memory_space=pltpu.VMEM)


def held(*shape, dtype=BF):
    return pltpu.VMEM(shape, dtype)


def keep(x):
    return pltpu.with_memory_space_constraint(x, pltpu.VMEM)


def leave(x):
    return pltpu.with_memory_space_constraint(x, pltpu.HBM)


def limit(mib):
    return pltpu.CompilerParams(vmem_limit_bytes=mib * 1024 * 1024)


def dot(left, right):
    return jnp.dot(left, right, preferred_element_type=F32)


def dot_t(left, right):
    return lax.dot_general(left, right, (((1,), (1,)), ((), ())), preferred_element_type=F32)


def dot_tl(left, right):
    return lax.dot_general(left, right, (((0,), (0,)), ((), ())), preferred_element_type=F32)


def columns(row):
    n = row.shape[1]
    return jnp.concatenate(
        [jnp.broadcast_to(row[:, s : s + 128], (128, 128)).T for s in range(0, n, 128)], axis=0
    )


def scale_rows(x, col):
    reps = x.shape[1] // 128
    return x * (jnp.tile(col, (1, reps)) if reps > 1 else col)


def count_tiles(dst_ref, nbrs, rows0, n_rows, weight=1.0):
    times = jnp.ones(nbrs.shape, jnp.int32)
    for k in range(1, 8):
        times = times + (nbrs == pltpu.roll(nbrs, k, 0)).astype(jnp.int32)
    times = times.astype(F32) * weight
    zero = jnp.zeros((16, 128), BF)
    sub = lax.broadcasted_iota(jnp.int32, (16, 128), 0)
    for c in range(0, nbrs.shape[1], 128):
        idx = [
            jnp.broadcast_to(nbrs[k : k + 1, c : c + 128], (16, 128)).astype(jnp.int16)
            for k in range(8)
        ]
        val = [jnp.broadcast_to(times[k : k + 1, c : c + 128], (16, 128)).astype(BF) for k in range(8)]

        def group(t, _):
            base = pl.multiple_of(t * 128, 128)
            first = (sub + (base + rows0)).astype(jnp.int16)
            for r in range(0, 128, 16):
                here = first + jnp.int16(r)
                acc = zero
                for k in range(8):
                    acc = jnp.where(idx[k] == here, val[k], acc)
                dst_ref[pl.ds(base + r, 16), c : c + 128] = acc
            return 0

        lax.fori_loop(0, n_rows // 128, group, 0)


def halo_kernel(hn_ref, hl_ref, bdeg_ref, hdeg_ref, g_hbm, h_hbm, p_ref, g_ref, h_ref, sems):
    copy_in = pltpu.make_async_copy(g_hbm, g_ref, sems.at[0])
    copy_in.start()
    nbrs = hn_ref[...]
    slot = lax.broadcasted_iota(jnp.int32, nbrs.shape, 0)
    nbrs = jnp.where(slot < hl_ref[...], nbrs, -1)
    count_tiles(h_ref, nbrs, 0, NH, lax.rsqrt(bdeg_ref[...].astype(F32)))
    copy_h = pltpu.make_async_copy(h_ref, h_hbm, sems.at[1])
    copy_h.start()
    inv_h = columns(lax.rsqrt(hdeg_ref[...].astype(F32)))
    copy_in.wait()
    p_ref[...] = scale_rows(dot(h_ref[...], g_ref[...]), inv_h).astype(BF)
    copy_h.wait()


def halo_call(hn, hl, bdeg, hdeg, g):
    return pl.pallas_call(
        halo_kernel,
        in_specs=[vmem_spec()] * 4 + [hbm_spec()],
        out_specs=[hbm_spec(), vmem_spec()],
        out_shape=(pltpu.HBM((NH, NB), BF), held(NH, HID)),
        scratch_shapes=[
            pltpu.VMEM((NB, HID), BF),
            pltpu.VMEM((NH, NB), BF),
            pltpu.SemaphoreType.DMA((2,)),
        ],
        compiler_params=limit(58),
        name="halo_part",
    )(hn, hl, bdeg, hdeg, leave(g))


def rows_of(ref, lo, hi):
    return ref[:, :, lo:hi].reshape(NH, hi - lo)


def chunks_of(x):
    return x.astype(BF).reshape(x.shape[0] // 4, 4, x.shape[1])


def selector(ask_ref, s_ref):
    a = ask_ref[...].reshape(64, 2, 1, 4)
    sub = lax.broadcasted_iota(jnp.int32, (64, 8, 4), 1)
    lane = lax.broadcasted_iota(jnp.int32, (64, 8, 4), 2)
    mine = jnp.where(
        sub < 4, jnp.broadcast_to(a[:, 0], (64, 8, 4)), jnp.broadcast_to(a[:, 1], (64, 8, 4))
    )
    mine = jnp.where(lane == (sub & 3), mine & (NB - 1), 0)
    col = jnp.sum(mine.astype(F32), axis=2, keepdims=True).reshape(512, 1).astype(jnp.int32)
    colb = jnp.broadcast_to(col, (512, 128)).reshape(64, 8, 128)
    lanes = lax.broadcasted_iota(jnp.int32, (1, 8, 128), 2)
    for c in range(0, NB, 128):
        s_ref[:, c : c + 128] = jnp.where(colb == lanes + c, 1.0, 0.0).reshape(512, 128).astype(BF)


def pick_kernel(
    ask_ref, x_hbm, e_ref, v_hbm, p_ref, out_hbm, s_ref, x_ref, v_ref, out_ref, sems
):
    copies = [
        pltpu.make_async_copy(src, dst, sems.at[n])
        for n, (src, dst) in enumerate(((v_hbm, v_ref), (x_hbm, x_ref)))
    ]
    for copy in copies:
        copy.start()
    out_ref[:, :, 1152:1664] = chunks_of(p_ref[...])
    selector(ask_ref, s_ref)
    s = s_ref[...]
    for n, (lo, hi, src) in enumerate(((128, 640, e_ref), (640, 1152, v_ref), (0, 128, x_ref))):
        if n:
            copies[n - 1].wait()
        out_ref[:, :, lo:hi] = chunks_of(dot(s, src[...]))
    send = pltpu.make_async_copy(out_ref, out_hbm, sems.at[2])
    send.start()
    send.wait()


def pick_call(asked, x, e, v, p):
    return pl.pallas_call(
        pick_kernel,
        in_specs=[vmem_spec(), hbm_spec(), vmem_spec(), hbm_spec(), vmem_spec()],
        out_specs=hbm_spec(),
        out_shape=pltpu.HBM((128, 4, 1664), BF),
        scratch_shapes=[
            pltpu.VMEM((NH, NB), BF),
            pltpu.VMEM((NB, FEAT), BF),
            pltpu.VMEM((NB, HID), BF),
            pltpu.VMEM((128, 4, 1664), BF),
            pltpu.SemaphoreType.DMA((3,)),
        ],
        compiler_params=limit(58),
        name="pick_rows",
    )(keep(asked), leave(x), keep(e), leave(v), keep(p))


def batch_kernel(
    nb_ref, bdeg_ref, f_ref, g_hbm, w2_ref, c_hbm, cf_ref, sp_hbm, bp_hbm,
    fs_ref, g_ref, gs_ref, c_ref, sp_ref, bp_ref, sems,
):
    copy_in = pltpu.make_async_copy(g_hbm, g_ref, sems.at[9])
    copy_in.start()
    col = columns(lax.rsqrt(bdeg_ref[...].astype(F32)))
    fs_ref[...] = (f_ref[...].astype(F32) * col).astype(BF)
    eye = (
        lax.broadcasted_iota(jnp.int32, (128, 128), 0)
        == lax.broadcasted_iota(jnp.int32, (128, 128), 1)
    ).astype(F32).astype(BF)
    count_tiles(c_ref, nb_ref[...], 0, NB)
    for r in range(0, NB, 128):
        c_ref[r : r + 128, r : r + 128] = c_ref[r : r + 128, r : r + 128] + eye
    copies = [pltpu.make_async_copy(c_ref, c_hbm, sems.at[0])]
    copies[0].start()
    copy_in.wait()
    for s in range(0, NB, STEP):
        gs = scale_rows(g_ref[s : s + STEP, :].astype(F32), col[s : s + STEP])
        gs_ref[s : s + STEP, :] = gs.astype(BF)
    for n, r in enumerate(range(0, NB, STEP)):
        at = slice(r, r + STEP)
        spread = dot(c_ref[at, :], gs_ref[...]).astype(BF)
        sp_ref[at, :] = spread
        bp_ref[at, :] = scale_rows(dot_t(spread, w2_ref[...]), col[at])
        for m, (src, dst) in enumerate(((sp_ref, sp_hbm), (bp_ref, bp_hbm))):
            copies.append(pltpu.make_async_copy(src.at[at], dst.at[at], sems.at[1 + 2 * n + m]))
            copies[-1].start()
        cf_ref[at, :] = dot_tl(c_ref[:, at], fs_ref[...]) * col[at]
    for copy in copies:
        copy.wait()


def batch_call(nb, bdeg, f, g, w2):
    return pl.pallas_call(
        batch_kernel,
        in_specs=[vmem_spec()] * 3 + [hbm_spec(), vmem_spec()],
        out_specs=[hbm_spec(), vmem_spec(), hbm_spec(), hbm_spec()],
        out_shape=(
            pltpu.HBM((NB, NB), BF),
            pltpu.HBM((NB, FEAT), F32),
            pltpu.HBM((NB, HID), BF),
            pltpu.HBM((NB, HID), F32),
        ),
        scratch_shapes=[
            pltpu.VMEM((NB, FEAT), BF),
            pltpu.VMEM((NB, HID), BF),
            pltpu.VMEM((NB, HID), BF),
            pltpu.VMEM((NB, NB), BF),
            pltpu.VMEM((NB, HID), BF),
            pltpu.VMEM((NB, HID), F32),
            pltpu.SemaphoreType.DMA((10,)),
        ],
        compiler_params=limit(58),
        name="batch_part",
    )(nb, bdeg, f, leave(g), w2)


def main_kernel(
    r_ref, h_hbm, cf_hbm, sp_hbm, bp_hbm, p_ref, w1_hbm, w2_hbm, bdeg_hbm, hdeg_hbm,
    hid_hbm, grads_ref,
    h_ref, cf_ref, sp_ref, bp_ref, w1_ref, w2_ref, bdeg_ref, hdeg_ref,
    hid_ref, mix_ref, g1_ref, g2_ref, sems,
):
    first = ((hdeg_hbm, hdeg_ref), (w2_hbm, w2_ref), (bdeg_hbm, bdeg_ref), (w1_hbm, w1_ref))
    copies = [pltpu.make_async_copy(src, dst, sems.at[n]) for n, (src, dst) in enumerate(first)]
    for copy in copies:
        copy.start()
    blocks = []
    for n, s in enumerate(range(0, NB, STEP)):
        at = slice(s, s + STEP)
        blocks.append([
            pltpu.make_async_copy(h_hbm.at[:, at], h_ref.at[:, at], sems.at[4 + 3 * n]),
            pltpu.make_async_copy(cf_hbm.at[at], cf_ref.at[at], sems.at[5 + 3 * n]),
            pltpu.make_async_copy(bp_hbm.at[at], bp_ref.at[at], sems.at[6 + 3 * n]),
        ])
    sp_copy = pltpu.make_async_copy(sp_hbm, sp_ref, sems.at[16])
    for copy in blocks[0]:
        copy.start()
    g2_ref[...] = dot_tl(rows_of(r_ref, 128, 640), p_ref[...])
    copies[0].wait()
    col_h = columns(lax.rsqrt(hdeg_ref[...].astype(F32)))
    mix_ref[:, 512:640] = (rows_of(r_ref, 0, 128).astype(F32) * col_h).astype(BF)
    copies[1].wait()
    mix_ref[:, 0:512] = scale_rows(dot_t(rows_of(r_ref, 640, 1152), w2_ref[...]), col_h).astype(BF)
    for block in blocks[1:]:
        for copy in block:
            copy.start()
    sp_copy.start()
    copies[2].wait()
    inv = columns(lax.rsqrt(bdeg_ref[...].astype(F32)))
    copies[3].wait()
    outs = []
    for n, s in enumerate(range(0, NB, STEP)):
        at = slice(s, s + STEP)
        blocks[n][0].wait()
        blocks[n][1].wait()
        h = h_ref[:, at]
        u1 = (cf_ref[at, :] + dot_tl(h, mix_ref[:, 512:640])).astype(BF)
        zh = 0.5 * dot(u1, w1_ref[...])
        t = jnp.tanh(zh)
        hid_ref[at, :] = (zh * scale_rows(1.0 + t, inv[at])).astype(BF)
        outs.append(pltpu.make_async_copy(hid_ref.at[at], hid_hbm.at[at], sems.at[17 + n]))
        outs[-1].start()
        slope = (0.5 + 0.5 * t) * (1.0 + zh * (1.0 - t))
        blocks[n][2].wait()
        d_pre = ((bp_ref[at, :] + dot_tl(h, mix_ref[:, 0:512])) * slope).astype(BF)
        g1 = dot_tl(u1, d_pre)
        if n == 0:
            g1_ref[...] = g1
        else:
            g1_ref[...] += g1
    sp_copy.wait()
    g2_ref[...] += dot_tl(hid_ref[...], sp_ref[...])
    grads_ref[:, :, 0:512] = chunks_of(g2_ref[...])
    for q in range(4):
        part = g1_ref[:, 128 * q : 128 * q + 128]
        grads_ref[32 * q : 32 * q + 32, :, 512:640] = chunks_of(part)
    for copy in outs:
        copy.wait()


def main_call(recv, h, cf, sp, bp, p, w1, w2, bdeg, hdeg):
    return pl.pallas_call(
        main_kernel,
        in_specs=[vmem_spec()] + [hbm_spec()] * 4 + [vmem_spec()] + [hbm_spec()] * 4,
        out_specs=[hbm_spec(), vmem_spec()],
        out_shape=(pltpu.HBM((NB, HID), BF), jax.ShapeDtypeStruct((128, 4, 640), BF)),
        scratch_shapes=[
            pltpu.VMEM((NH, NB), BF),
            pltpu.VMEM((NB, FEAT), F32),
            pltpu.VMEM((NB, HID), BF),
            pltpu.VMEM((NB, HID), F32),
            pltpu.VMEM((FEAT, HID), BF),
            pltpu.VMEM((HID, HID), BF),
            pltpu.VMEM((1, NB), jnp.int32),
            pltpu.VMEM((1, NH), jnp.int32),
            pltpu.VMEM((NB, HID), BF),
            pltpu.VMEM((NH, HID + FEAT), BF),
            pltpu.VMEM((FEAT, HID), F32),
            pltpu.VMEM((HID, HID), F32),
            pltpu.SemaphoreType.DMA((21,)),
        ],
        compiler_params=limit(58),
        name="main_part",
    )(keep(recv), leave(h), leave(cf), leave(sp), leave(bp), keep(p), leave(w1), leave(w2), leave(bdeg), leave(hdeg))


def out_kernel(half, refs):
    r_ref, c_hbm, h_hbm, hid_ref, w2_ref, bdeg_ref, hdeg_ref = refs[:7]
    out_hbm, c_ref, h_ref, he_ref, out_ref, sems = refs[-6:]
    at = slice(half * NB // 2, (half + 1) * NB // 2)
    ins = [
        pltpu.make_async_copy(c_hbm.at[:, at], c_ref, sems.at[0]),
        pltpu.make_async_copy(h_hbm.at[:, at], h_ref, sems.at[1]),
    ]
    for copy in ins:
        copy.start()
    inv = columns(lax.rsqrt(bdeg_ref[:, at].astype(F32)))
    col_h = columns(lax.rsqrt(hdeg_ref[...].astype(F32)))
    he_ref[...] = scale_rows(rows_of(r_ref, 128, 640).astype(F32), col_h).astype(BF)
    for copy in ins:
        copy.wait()
    outs = []
    for n, s in enumerate(range(0, NB // 2, STEP)):
        here = slice(s, s + STEP)
        there = slice(at.start + s, at.start + s + STEP)
        own = scale_rows(dot_tl(c_ref[:, here], hid_ref[...]), inv[here])
        u = (own + dot_tl(h_ref[:, here], he_ref[...])).astype(BF)
        out_ref[here] = dot(u, w2_ref[...]).astype(BF)
        outs.append(pltpu.make_async_copy(out_ref.at[here], out_hbm.at[there], sems.at[2 + n]))
        outs[-1].start()
    for copy in outs:
        copy.wait()


def out_call(half, recv, c, h, hid, w2, bdeg, hdeg, *first):
    return pl.pallas_call(
        lambda *refs: out_kernel(half, refs),
        in_specs=[vmem_spec(), hbm_spec(), hbm_spec()] + [vmem_spec()] * 4 + [hbm_spec()] * len(first),
        out_specs=hbm_spec(),
        out_shape=pltpu.HBM((NB, HID), BF),
        input_output_aliases={7: 0} if first else {},
        scratch_shapes=[
            pltpu.VMEM((NB, NB // 2), BF),
            pltpu.VMEM((NH, NB // 2), BF),
            pltpu.VMEM((NH, HID), BF),
            pltpu.VMEM((NB // 2, HID), BF),
            pltpu.SemaphoreType.DMA((4,)),
        ],
        compiler_params=limit(58),
        name=f"out_part_{half}",
    )(keep(recv), leave(c), leave(h), hid, w2, bdeg, hdeg, *first)


def tail_kernel(ask_ref, r_ref, hg_hbm, s_ref, pa_ref, hg_ref, sems):
    selector(ask_ref, s_ref)
    pa_ref[...] = rows_of(r_ref, 1152, 1664)
    copies = []
    for n, r in enumerate(range(0, NB, STEP)):
        at = slice(r, r + STEP)
        hg_ref[at] = dot_tl(s_ref[:, at], pa_ref[...]).astype(BF)
        copies.append(pltpu.make_async_copy(hg_ref.at[at], hg_hbm.at[at], sems.at[n]))
        copies[-1].start()
    for copy in copies:
        copy.wait()


def tail_call(asked, recv):
    return pl.pallas_call(
        tail_kernel,
        in_specs=[vmem_spec()] * 2,
        out_specs=hbm_spec(),
        out_shape=jax.ShapeDtypeStruct((NB, HID), BF),
        scratch_shapes=[
            pltpu.VMEM((NH, NB), BF),
            pltpu.VMEM((NH, HID), BF),
            pltpu.VMEM((NB, HID), BF),
            pltpu.SemaphoreType.DMA((4,)),
        ],
        compiler_params=limit(58),
        name="tail_part",
    )(keep(asked), keep(recv))


def sum_kernel(x_ref, o_ref):
    total = jnp.sum(x_ref[...].astype(F32), axis=0)
    o_ref[...] = jnp.broadcast_to(total.astype(BF)[None], (128, 4, 640))


def sum_call(x):
    return pl.pallas_call(
        sum_kernel,
        in_specs=[vmem_spec()],
        out_specs=vmem_spec(),
        out_shape=jax.ShapeDtypeStruct((128, 4, 640), BF),
        name="sum_part",
    )(keep(x))


def final_kernel(x_ref, g1_ref, g2_ref):
    factor = 1.0 / 512.0
    g2_ref[...] = rows_of(x_ref, 0, 512).astype(F32) * factor
    for q in range(4):
        part = x_ref[32 * q : 32 * q + 32, :, 512:640].reshape(128, 128)
        g1_ref[:, 128 * q : 128 * q + 128] = part.astype(F32) * factor


def final_call(x):
    return pl.pallas_call(
        final_kernel,
        in_specs=[vmem_spec()],
        out_specs=[vmem_spec()] * 2,
        out_shape=(
            jax.ShapeDtypeStruct((FEAT, HID), F32),
            jax.ShapeDtypeStruct((HID, HID), F32),
        ),
        name="final_part",
    )(keep(x))


def exchange(x):
    return lax.all_to_all(x, AXES, split_axis=0, concat_axis=0, tiled=True)


def local(
    node_feats, batch_deg, batch_nbrs, halo_nbrs, halo_len, halo_rows, halo_deg,
    feat_table, emb_table, grad_table, weight_one, weight_two, grad_out,
):
    bdeg = batch_deg.reshape(1, NB)
    hdeg = halo_deg.reshape(1, NH)
    asked = exchange(halo_rows.reshape(128, 1, 4))
    h, p = halo_call(halo_nbrs.T, halo_len.reshape(1, NB), bdeg, hdeg, grad_out)
    send = pick_call(asked, feat_table, emb_table, grad_table, p)
    recv = exchange(send)
    c, cf, sp, bp = batch_call(batch_nbrs.T, bdeg, node_feats, grad_out, weight_two)
    hid, grads = main_call(recv, h, cf, sp, bp, p, weight_one, weight_two, bdeg, hdeg)
    shares = exchange(grads)
    half = out_call(0, recv, c, h, hid, weight_two, bdeg, hdeg)
    shares, half = lax.optimization_barrier((shares, half))
    sums = exchange(sum_call(shares))
    out_embed = out_call(1, recv, c, h, hid, weight_two, bdeg, hdeg, half)
    halo_grad = tail_call(asked, recv)
    grad_one, grad_two = final_call(sums)
    return out_embed, halo_grad, grad_one, grad_two


def solution(mesh):
    rows = P(AXES, None)
    flat = P(AXES)
    return jax.shard_map(
        local,
        mesh=mesh,
        in_specs=(
            rows, flat, rows, rows, flat, flat, flat, rows, rows, rows, P(), P(), rows,
        ),
        out_specs=(rows, rows, P(), P()),
        check_vma=False,
    )
```
